512 devices in a mesh: gx: 16 (over z), gy: 32 (over y, x, core).
Axes of the slice: x: 4, y: 4, z: 16, core: 2. Of those that a mesh axis runs over, the one named last changes fastest.
Arguments:
- noise: float32 [16, 512, 512], P('gx', 'gy'), may hold values from -6 to 6
- stencil: float32 [9], replicated, may hold values from 0.04 to 0.2
- mean_counts: float32 [4], replicated, may hold values from 0.5 to 4
- bias_one: float32 [4], replicated, may hold values from 1 to 2
- bias_two: float32 [4], replicated, may hold values from 0.05 to 0.3
- owner: int32 [32, 16, 4, 1], P('gy', 'gx'), may hold values from 0 to 15; in each aligned block of 4 rows (0 to 3, 4 to 7, ..., all dimensions but the last counted through in order) at most 2 rows name the same one
- depth: int32 [16, 32, 32], P('gx', None, 'gy'), may hold values from 0 to 3
- counts: int32 [16, 32, 32, 16, 128], P('gx', None, 'gy'), may hold values from 0 to 6
Outputs:
- gradient: float32 [16, 512, 512], P('gx', 'gy')
- density: float32 [16, 512, 512], P('gx', 'gy')
The draws below stay inside these ranges and needn't reach their ends.
Inputs may be any that keep to these rules, and one draw needn't show every extreme that they name: Of the tiles of one device (aligned blocks of 4 rows), at most 2 name the same owner, and in every draw some owner is named exactly 2 times by one device.
All inputs are finite; a program needn't handle non-finite values.
Results may differ from the reference program's by a relative error of at most 0.0001.
Values sent between devices are 32-bit elements; how exact they have to be, the bound alone decides.
A program may use at most 64 MiB of HBM per device.

```python
import math
import jax
import jax.numpy as jnp
import numpy as np
from jax import lax

NG = 512
TC = 128
DEPTHS = 4
PL = 16
XL = 16
NT = 4
TILES_DEV = 4
CAP = 2
SLOTS = 32
N_GX = 16
N_GY = 32


def place_ends(result, own_key, least, high):
    place = [jax.random.randint(jax.random.fold_in(own_key, axis), (), 0, length) for axis, length in enumerate(result.shape)]
    longest = result.shape.index(max(result.shape))
    beside = place[:longest] + [(place[longest] + 1) % result.shape[longest]] + place[longest + 1:]
    return result.at[tuple(place)].set(least).at[tuple(beside)].set(high)


def levels(stream_key, extent, cuts, smallest, high):
    def one(dim, parts):
        heights = jax.random.uniform(jax.random.fold_in(jax.random.fold_in(stream_key, 6), dim), (parts,), jnp.float32, smallest / len(cuts), high / len(cuts))
        return jnp.repeat(jnp.exp(heights), extent[dim] // parts).reshape((-1,) + (1,) * (len(extent) - dim - 1))

    level = one(*cuts[0])
    for cut in cuts[1:]:
        level = level * one(*cut)
    return level


def routed_block(key, own, number, rows, amount, top, bound, skew):
    ranking = jax.random.permutation(key, amount)
    heavy_load, common = portions_of(amount, rows * top, bound, skew, True), portions_of(amount, rows * top, bound, skew, False)
    places = jnp.arange(amount)

    def named(tallies, turn):
        used = int((tallies > 0).sum())
        fixed = max(1, used // 4)
        shifted = fixed + (places - fixed + turn * (used - fixed)) % max(1, amount - fixed)
        return jnp.zeros((amount,), jnp.int32).at[ranking[jnp.where(places < fixed, places, shifted)]].set(jnp.asarray(tallies, jnp.int32))

    tallies = jnp.where(number % 4 == 0, named(heavy_load, number // 4), named(common, number - number // 4 - 1))
    mixed = jax.random.permutation(jax.random.fold_in(own, 3), amount)
    donor, sink = mixed[0:amount // 2 * 2:2], mixed[1:amount // 2 * 2:2]
    slack = jnp.minimum(tallies[donor] - 1, bound - tallies[sink]) // 2
    slack = jnp.where((donor == ranking[0]) | (sink == ranking[0]) | (tallies[sink] == 0), 0, jnp.maximum(slack, 0))
    shifted = jax.random.randint(jax.random.fold_in(own, 4), (amount // 2,), 0, 1 << 20) % (slack + 1)
    tallies = tallies.at[donor].add(-shifted).at[sink].add(shifted)
    items = jnp.searchsorted(jnp.cumsum(tallies), jnp.arange(rows * top), side="right").astype(jnp.int32)
    grid = items.reshape(top, rows).T
    grid = grid[jax.random.permutation(jax.random.fold_in(own, 1), rows)]
    turn = jax.random.randint(jax.random.fold_in(own, 2), (rows, 1), 0, top)
    return jnp.take_along_axis(grid, (jnp.arange(top)[None, :] + turn) % top, axis=1)


def portions_of(number_of, total, limit, skew, full):
    loads = [(1 << 20) // math.isqrt(rank ** skew) + 1 for rank in range(1, number_of + 1)]
    largest = limit if full else min(limit, max(-(-total // number_of), total * loads[0] // sum(loads)))
    least = 1 if total - largest >= number_of - 1 else 0
    holding, rest = [largest] + [least] * (number_of - 1), total - largest - least * (number_of - 1)
    while rest > 0:
        candidates = [i for i in range(1, number_of) if holding[i] < largest] or [i for i in range(1, number_of) if holding[i] < limit]
        whole, remaining = sum([loads[i] for i in candidates]), rest
        for i in candidates:
            more = min(limit - holding[i], max(1, remaining * loads[i] // whole), rest)
            holding[i] = holding[i] + more
            rest = rest - more
    return np.array(holding)


def centred(key, extent, deviation, reach, split=(), held_as=jnp.bfloat16):
    drawn = jax.random.normal(key, extent, jnp.float32) * deviation
    if len(split) > 0:
        drawn = levels(key, extent, split, -0.22, 0.18) * drawn
    return jnp.clip(drawn, min=-reach, max=reach).astype(held_as)


def setup_inputs(seed: int = 0) -> dict:
    streams_of = jax.random.split(jax.random.key(seed), 9)
    noise = centred(streams_of[0], (PL, NG, NG), 1.0, 6.0, ((0, 16), (1, 32)), jnp.float32)
    stencil = jnp.clip(jax.random.uniform(streams_of[1], (9,), jnp.float32, 0.04, 0.2), 0.04, 0.2)
    mean_counts = jnp.clip(jnp.exp(jax.random.uniform(streams_of[2], (DEPTHS,), jnp.float32, math.log(0.5), math.log(4.0))), 0.5, 4.0)
    bias_one = jnp.clip(jax.random.uniform(streams_of[3], (DEPTHS,), jnp.float32, 1.0, 2.0), 1.0, 2.0)
    bias_two = jnp.clip(jax.random.uniform(streams_of[4], (DEPTHS,), jnp.float32, 0.05, 0.3), 0.05, 0.3)
    owner_keys = jax.random.split(jax.random.fold_in(streams_of[5], 1), N_GY * PL * NT // TILES_DEV)
    owner_turns = jax.random.permutation(jax.random.fold_in(streams_of[5], 3), N_GY * PL * NT // TILES_DEV)
    owner = jax.vmap(lambda own, number: routed_block(jax.random.fold_in(streams_of[5], 2), own, number, TILES_DEV, N_GX, 1, CAP, 2))(owner_keys, owner_turns).reshape((N_GY, PL, NT, 1))
    depth = place_ends(jax.random.randint(streams_of[6], (N_GX, SLOTS, N_GY), 0, DEPTHS), jax.random.fold_in(streams_of[6], 1), 0, DEPTHS - 1).astype(jnp.int32)
    counts = place_ends(jax.random.randint(streams_of[7], (N_GX, SLOTS, N_GY, XL, TC), 0, 7), jax.random.fold_in(streams_of[7], 1), 0, 6).astype(jnp.int32)
    return {"noise": noise, "stencil": stencil, "mean_counts": mean_counts, "bias_one": bias_one, "bias_two": bias_two, "owner": owner, "depth": depth, "counts": counts}


AMPLITUDE = 0.75
PIVOT = 1.0
GROWTH = 7.0 / 8.0

def spectra_tables():
    steps_all = jnp.fft.fftfreq(NG) * NG
    wave_x = 2.0 * math.pi / NG * steps_all[:, None]
    wave_y = 2.0 * math.pi / NG * steps_all[None, :]
    wave_sq = wave_x * wave_x + wave_y * wave_y
    keep_mask = (jnp.abs(steps_all)[:, None] * 2 != NG) & (jnp.abs(steps_all)[None, :] * 2 != NG)
    wave_safe = jnp.where(wave_sq > 0, wave_sq, 1.0)
    inverse_sq = jnp.where(wave_sq > 0, 1.0 / wave_safe, 0.0)
    envelope = jnp.where(keep_mask, AMPLITUDE * (jnp.sqrt(wave_sq) / PIVOT) / (1.0 + wave_sq / (PIVOT * PIVOT)), 0.0)
    factors = [jnp.ones_like(wave_sq), wave_x * inverse_sq, wave_y * inverse_sq, wave_x, wave_y]
    return (envelope, factors)

def stencil_sum(field, weights, orient):
    summed = jnp.zeros_like(field)
    for step_x in (-1, 0, 1):
        for step_y in (-1, 0, 1):
            summed = summed + weights[(step_x + 1) * 3 + step_y + 1] * jnp.roll(field, (-orient * step_x, -orient * step_y), axis=(1, 2))
    return summed

def reference(noise, stencil, mean_counts, bias_one, bias_two, owner, depth, counts):
    envelope, factors = spectra_tables()
    wave_modes = jnp.fft.fft2(noise, axes=(1, 2)) * envelope
    fields = []
    for field_index in range(5):
        if field_index == 0:
            spectrum = wave_modes
        else:
            spectrum = 1j * factors[field_index] * wave_modes
        fields.append(jnp.real(jnp.fft.ifft2(spectrum, axes=(1, 2))).astype(jnp.float32))
    linear, shift_x, shift_y, slope_x, slope_y = fields
    density = linear + GROWTH * linear * linear - (shift_x * slope_x + shift_y * slope_y)
    smooth = stencil_sum(density, stencil, 1)
    tile_vals = smooth.reshape(PL, N_GY, XL, NT, TC).transpose(1, 0, 3, 2, 4).reshape(N_GY, N_GX, TILES_DEV, XL, TC)
    dest_owner = owner.reshape(N_GY, N_GX, TILES_DEV)
    onehot = (dest_owner[..., None] == jnp.arange(N_GX, dtype=jnp.int32)).astype(jnp.int32)
    rank_in = lax.optimization_barrier(jnp.sum((jnp.cumsum(onehot, axis=2) - onehot) * onehot, axis=3))
    slot_index = jnp.arange(N_GX, dtype=jnp.int32)[None, :, None] * CAP + rank_in
    column = jnp.broadcast_to(jnp.arange(N_GY, dtype=jnp.int32)[:, None, None], dest_owner.shape)
    cell_counts = counts[dest_owner, slot_index, column].astype(jnp.float32)
    classes = depth[dest_owner, slot_index, column]
    level_mean = mean_counts[classes][..., None, None]
    bias_lin = bias_one[classes][..., None, None]
    bias_sq = bias_two[classes][..., None, None]
    rate_cell = level_mean * jnp.exp(bias_lin * tile_vals + bias_sq * tile_vals * tile_vals)
    score_tile = (cell_counts - rate_cell) * (bias_lin + 2.0 * bias_sq * tile_vals)
    score_field = score_tile.reshape(N_GY, PL, NT, XL, TC).transpose(1, 0, 3, 2, 4).reshape(PL, NG, NG)
    pulled = stencil_sum(score_field, stencil, -1)
    adjoints = [pulled * (1.0 + 2.0 * GROWTH * linear), -pulled * slope_x, -pulled * slope_y, -pulled * shift_x, -pulled * shift_y]
    summed = jnp.fft.fft2(adjoints[0], axes=(1, 2))
    for field_index in range(1, 5):
        summed = summed - 1j * factors[field_index] * jnp.fft.fft2(adjoints[field_index], axes=(1, 2))
    pulled_back = jnp.real(jnp.fft.ifft2(envelope * summed, axes=(1, 2))).astype(jnp.float32)
    return (pulled_back - noise, density)
```

```python
import functools
import math

import jax
import jax.numpy as jnp
import ml_dtypes
import numpy as np
from jax import lax
from jax.experimental import pallas as pl
from jax.experimental.pallas import tpu as pltpu
from jax.sharding import PartitionSpec as P

MESH = pl.DeviceIdType.MESH
NG = 512
TC = 128
NT = 4
AMPLITUDE = 0.75
GROWTH = 7.0 / 8.0
UNIT = 2.0 * math.pi / NG
F32 = jnp.float32
BF16 = jnp.bfloat16


def halves(table):
    high = table.astype(ml_dtypes.bfloat16)
    low = (table - high.astype(np.float64)).astype(ml_dtypes.bfloat16)
    return high, low


def make_tables():
    y = np.arange(256)[:, None]
    lane = np.arange(256)[None, :]
    half = 8 * (lane // 16) + lane % 8
    part = (lane // 8) % 2
    w = []
    for odd in (0, 1):
        turn = (y * (2 * half + odd)) % NG
        w.append(np.where(part == 0, np.cos(UNIT * turn), -np.sin(UNIT * turn)))
    w_tab = np.stack([piece for table in w for piece in halves(table)])
    k = np.arange(64)[:, None]
    row = np.arange(64)[None, :]
    turn = (k * (2 * (row % 32) + row // 32)) % 64
    cs = np.concatenate([np.cos(2 * math.pi * turn / 64), np.sin(2 * math.pi * turn / 64)], 0)
    hi, lo = halves(cs)
    cs_tab = np.concatenate([hi, lo, hi], 1)
    hi, lo = halves(np.concatenate([cs[:64].T, cs[64:].T], 1))
    ct_tab = np.concatenate([hi, lo, hi], 1)
    d8 = np.zeros((8, 2, 8, 8, 2, 8))
    for xl in range(8):
        for q in range(8):
            co, si = np.cos(2 * math.pi * (q * xl % 8) / 8), np.sin(2 * math.pi * (q * xl % 8) / 8)
            for m in range(8):
                d8[xl, 0, m, q, 0, m] = co
                d8[xl, 1, m, q, 0, m] = si
                d8[xl, 1, m, q, 1, m] = co
                d8[xl, 0, m, q, 1, m] = -si
    d8 = d8.reshape(128, 128)
    minus_i = np.zeros((128, 128))
    for g in range(8):
        for m in range(8):
            minus_i[g * 16 + 8 + m, g * 16 + m] = 1.0
            minus_i[g * 16 + m, g * 16 + 8 + m] = -1.0
    d8_tab = np.stack(halves(np.concatenate([d8, minus_i @ d8], 0)))
    kk = np.arange(64)[:, None]
    xl = (np.arange(128) // 16)[None, :]
    tw_tab = np.stack([np.cos(UNIT * kk * xl), np.sin(UNIT * kk * xl)]).astype(np.float32)
    return w_tab, cs_tab, ct_tab, d8_tab, tw_tab


def split(x):
    high = x.astype(BF16)
    return high, (x - high.astype(F32)).astype(BF16)


def nn(a, b):
    return lax.dot_general(a, b, (((1,), (0,)), ((), ())), preferred_element_type=F32)


def nt(a, b):
    return lax.dot_general(a, b, (((1,), (1,)), ((), ())), preferred_element_type=F32)


def dot3(mul, x, high, low):
    x_high, x_low = split(x)
    return mul(x_high, high) + (mul(x_high, low) + mul(x_low, high))


def left3(table, x):
    x_high, x_low = split(x)
    return nn(table, jnp.concatenate([x_high, x_high, x_low], 0))


def rows_forward(v, w):
    low, high = v[:, :256], v[:, 256:]
    return jnp.concatenate([dot3(nn, low + high, w[0], w[1]), dot3(nn, low - high, w[2], w[3])], 1)


def rows_inverse(s, w):
    even, odd = dot3(nt, s[:, :256], w[0], w[1]), dot3(nt, s[:, 256:], w[2], w[3])
    return jnp.concatenate([even + odd, even - odd], 1)


def columns_forward(fields, cs, d8, tw):
    turned = left3(cs, jnp.concatenate(fields, 1))
    tc, ts = tw
    parts = []
    for f in range(len(fields)):
        a, b = turned[:64, 128 * f : 128 * f + 128], turned[64:, 128 * f : 128 * f + 128]
        parts.append(jnp.concatenate([tc * a - ts * b, tc * b + ts * a], 1))
    out = dot3(nn, jnp.concatenate(parts, 0), d8[0], d8[1])
    return [out[64 * f : 64 * f + 64] for f in range(len(fields))]


def columns_inverse(fields, ct, d8, tw):
    out = dot3(nt, jnp.concatenate(fields, 0), d8[0], d8[1])
    tc, ts = tw
    parts = []
    for f in range(len(fields)):
        a, b = out[64 * f : 64 * f + 64, :128], out[64 * f : 64 * f + 64, 128:]
        parts.append(jnp.concatenate([tc * a + ts * b, tc * b - ts * a], 0))
    back = left3(ct, jnp.concatenate(parts, 1))
    return [back[:, 128 * f : 128 * f + 128] for f in range(len(fields))]


def swap_parts(v, roll):
    lane = lax.broadcasted_iota(jnp.int32, v.shape, 1)
    return jnp.where(lane // 8 % 2 == 0, roll(v, v.shape[1] - 8, 1), roll(v, 8, 1))


def part_sign(shape):
    lane = lax.broadcasted_iota(jnp.int32, shape, 1)
    return jnp.where(lane // 8 % 2 == 0, -1.0, 1.0).astype(F32)


def times_ky(v, roll):
    lane = lax.broadcasted_iota(jnp.int32, (1, NG), 1)
    e = lane // 16
    ky = UNIT * (2 * (8 * (e % 16) + lane % 8) + e // 16).astype(F32)
    return part_sign((1, NG)) * ky * swap_parts(v, roll)


def filters(e):
    shape = (64, 128)
    k = lax.broadcasted_iota(jnp.int32, shape, 0)
    lane = lax.broadcasted_iota(jnp.int32, shape, 1)
    mx = k + 64 * (lane // 16)
    my = 2 * (8 * (e % 16) + lane % 8) + e // 16
    kx = UNIT * jnp.where(mx > NG // 2, mx - NG, mx).astype(F32)
    ky = UNIT * my.astype(F32)
    k2 = kx * kx + ky * ky
    safe = jnp.where(k2 > 0, k2, 1.0)
    inverse_sq = jnp.where(k2 > 0, 1.0 / safe, 0.0)
    envelope = jnp.where(mx != NG // 2, AMPLITUDE * jnp.sqrt(k2) / (1.0 + k2), 0.0)
    weight = jnp.where(my == 0, 1.0, 2.0).astype(F32) / (NG * NG)
    base = weight * envelope
    return base, base * kx * inverse_sq, base * kx, base * inverse_sq


def turn_vreg(x, roll):
    row = lax.broadcasted_iota(jnp.int32, (8, 128), 0)
    group = lax.broadcasted_iota(jnp.int32, (8, 128), 1) // 16
    for s in (1, 2, 4):
        row_bit, group_bit = row // s % 2, group // s % 2
        down = roll(roll(x, 8 - s, 0), 16 * s, 1)
        up = down if s == 4 else roll(roll(x, s, 0), 128 - 16 * s, 1)
        x = jnp.where(row_bit == group_bit, x, jnp.where(row_bit == 0, down, up))
    return x


def turn_list(vs, roll):
    group = lax.broadcasted_iota(jnp.int32, vs[0].shape, 1) // 16
    vs = list(vs)
    for s in (1, 2, 4):
        low = group // s % 2 == 0
        for i in range(8):
            if i & s == 0:
                a, b = vs[i], vs[i + s]
                vs[i] = jnp.where(low, a, roll(b, 16 * s, 1))
                vs[i + s] = jnp.where(low, roll(a, 128 - 16 * s, 1), b)
    return vs


def panels(nat, start, stop):
    return jnp.concatenate([nat[72 * eb + start : 72 * eb + stop, :] for eb in range(4)], 1)


def halo_out(backs, roll):
    group = lax.broadcasted_iota(jnp.int32, (32, 128), 1) // 16
    before = after = jnp.zeros((32, 128), F32)
    for f, back in enumerate(backs):
        before = jnp.where(group == 2 * f, roll(back[32:], 16 * ((2 * f - 7) % 8), 1), before)
        shifted = roll(back[:32], 16 * (2 * f + 1), 1)
        after = jnp.where(group == 2 * f + 1, shifted, after)
    return jnp.where(group % 2 == 0, roll(before, 1, 0), roll(after, 31, 0))


def halo_in(mains, halo, roll):
    group = lax.broadcasted_iota(jnp.int32, (32, 128), 1) // 16
    from_next, from_prev = roll(halo, 31, 0), roll(halo, 1, 0)
    out = []
    for f, main in enumerate(mains):
        top = main[:32] + jnp.where(group == 0, roll(from_prev, 16 * ((8 - 2 * f - 1) % 8), 1), 0.0)
        end = main[32:] + jnp.where(group == 7, roll(from_next, 16 * (7 - 2 * f), 1), 0.0)
        out.append(jnp.concatenate([top, end], 0))
    return out


def spread(nat, halo, w, roll):
    rows = [nat[0:48], times_ky(nat[48:64], roll), times_ky(nat[0:16], roll), halo, times_ky(halo, roll)]
    return rows_inverse(jnp.concatenate(rows, 0), w)


def field_rows(out):
    main = (out[0:16], out[16:32], out[32:48], out[48:64], out[64:80])
    edge = (out[80:82], out[82:84], out[84:86], out[94:96], out[88:90])
    return main, edge


def density_of(fields):
    linear, shift_x, slope_x, shift_y, slope_y = fields
    return linear + GROWTH * linear * linear - (shift_x * slope_x + shift_y * slope_y)


def adjoints_of(pulled, fields):
    linear, shift_x, slope_x, shift_y, slope_y = fields
    return (
        pulled * (1.0 + 2.0 * GROWTH * linear),
        -pulled * slope_x,
        -pulled * shift_x,
        -pulled * slope_y,
        -pulled * shift_y,
    )


def adjoint_rows(main, edge, w, roll):
    none = jnp.zeros((2, NG), F32)
    rows = list(main) + [edge[0], edge[1], edge[2], none, edge[4], none, none, edge[3]]
    out = rows_forward(jnp.concatenate(rows, 0), w)
    nat = jnp.concatenate(
        [out[0:16] - times_ky(out[64:80], roll), out[16:48], -times_ky(out[48:64], roll)], 0
    )
    return nat, out[80:88] - times_ky(out[88:96], roll)


def kernel(
    n_gx, n_gy, noise_ref, stencil_ref, mean_ref, one_ref, two_ref, owner_ref, depth_ref, counts_ref,
    w_ref, cs_ref, ct_ref, d8_ref, tw_ref, grad_ref, dens_ref,
    s1, r1, s2, r2, s3, r3, s4, r4, nat, field, frame, dsend, dgot, cgot,
    send_sem, recv_sem, zsend_sem, zrecv_sem,
):
    roll = pltpu.roll
    gx, gy = lax.axis_index("gx"), lax.axis_index("gy")

    barrier = pltpu.get_barrier_semaphore()

    @pl.loop(1, n_gy)
    def _(off):
        pl.semaphore_signal(barrier, inc=1, device_id=(gx, lax.rem(gy + off, n_gy)), device_id_type=MESH)

    @pl.loop(1, n_gx)
    def _(off):
        pl.semaphore_signal(barrier, inc=1, device_id=(lax.rem(gx + off, n_gx), gy), device_id_type=MESH)

    def exchange(phase, src, dst, pitch, count):
        @pl.loop(1, n_gy)
        def _(off):
            to = lax.rem(gy + off, n_gy)
            pltpu.make_async_remote_copy(
                src_ref=src.at[pl.ds(pl.multiple_of(to * pitch, 8), count)],
                dst_ref=dst.at[pl.ds(pl.multiple_of(gy * pitch, 8), count)],
                send_sem=send_sem.at[phase],
                recv_sem=recv_sem.at[phase],
                device_id=(gx, to),
                device_id_type=MESH,
            ).start()

        mine = pl.ds(pl.multiple_of(gy * pitch, 8), pitch)
        dst[mine, :] = src[mine, :]

    def everything(phase, buf, count):
        rows = pl.ds(0, (n_gy - 1) * count)
        return pltpu.make_async_remote_copy(
            src_ref=buf.at[rows],
            dst_ref=buf.at[rows],
            send_sem=send_sem.at[phase],
            recv_sem=recv_sem.at[phase],
            device_id=(gx, lax.rem(gy + 1, n_gy)),
            device_id_type=MESH,
        )

    w = [w_ref.at[i] for i in range(4)]
    w = [ref[...] for ref in w]

    spec = rows_forward(noise_ref[...], w)
    for xh in range(2):
        for eb in range(4):
            block = spec[8 * xh : 8 * xh + 8, 128 * eb : 128 * eb + 128]
            s1[pl.ds(64 * eb + xh, 8, stride=8), :] = turn_vreg(block, roll)
    wide = jnp.broadcast_to(depth_ref[...], (2 * n_gx, 128))
    for slot in range(2 * n_gx):
        dsend[slot // 2, slot % 2 : slot % 2 + 1, :] = wide[slot : slot + 1, :]

    pl.semaphore_wait(barrier, n_gy - 1 + n_gx - 1)
    exchange(0, s1, r1, 8, 2)

    @pl.loop(1, n_gx)
    def _(off):
        to = lax.rem(gx + off, n_gx)
        pltpu.make_async_remote_copy(
            src_ref=counts_ref.at[pl.ds(2 * to, 2)],
            dst_ref=cgot.at[pl.ds(2 * gx, 2)],
            send_sem=zsend_sem.at[0],
            recv_sem=zrecv_sem.at[0],
            device_id=(to, gy),
            device_id_type=MESH,
        ).start()
        pltpu.make_async_remote_copy(
            src_ref=dsend.at[to],
            dst_ref=dgot.at[gx],
            send_sem=zsend_sem.at[1],
            recv_sem=zrecv_sem.at[1],
            device_id=(to, gy),
            device_id_type=MESH,
        ).start()

    own = pltpu.make_async_copy(counts_ref.at[pl.ds(2 * gx, 2)], cgot.at[pl.ds(2 * gx, 2)], zsend_sem.at[2])
    own.start()
    dgot[gx] = dsend[gx]

    flt = filters(gy)
    tw = (tw_ref[0], tw_ref[1])
    d8 = (d8_ref[0], d8_ref[1])
    cs, ct = cs_ref[...], ct_ref[...]
    sign = part_sign((64, 128))

    everything(0, r1, 2).wait_recv()
    packed = jnp.concatenate([r1[pl.ds(xh, 32, stride=8), :] for xh in range(2)], 0)
    modes = columns_forward([packed], cs, d8, tw)[0]
    turned = sign * swap_parts(modes, roll)
    backs = columns_inverse([flt[0] * modes, flt[1] * turned, flt[2] * turned, flt[3] * modes], ct, d8, tw)
    for f in range(4):
        for xh in range(2):
            s2[pl.ds(2 * f + xh, 32, stride=16), :] = backs[f][32 * xh : 32 * xh + 32]
    s2[pl.ds(8, 32, stride=16), :] = halo_out(backs, roll)
    exchange(1, s2, r2, 16, 9)

    everything(1, r2, 9).wait_recv()
    for eb in range(4):
        outs = turn_list([r2[128 * eb + 16 * i : 128 * eb + 16 * i + 8, :] for i in range(8)], roll)
        for xl in range(8):
            nat[pl.ds(72 * eb + xl, 8, stride=8), :] = outs[xl]
        nat[72 * eb + 64 : 72 * eb + 72, :] = turn_vreg(r2[pl.ds(128 * eb + 8, 8, stride=16), :], roll)
    field[...] = spread(panels(nat, 0, 64), panels(nat, 64, 72), w, roll)
    main, edge = field_rows(field)
    dens = density_of(main)
    dens_edge = density_of(edge)
    dens_ref[...] = dens
    frame[8:24, :] = dens
    frame[7:8, :] = dens_edge[0:1]
    frame[24:25, :] = dens_edge[1:2]
    cols = []
    for b in range(3):
        cols.append(sum(stencil_ref[3 * a + b] * frame[7 + a : 23 + a, :] for a in range(3)))
    smooth = roll(cols[0], 1, 1) + cols[1] + roll(cols[2], NG - 1, 1)

    got = pltpu.make_async_remote_copy(
        src_ref=cgot.at[pl.ds(0, 2 * n_gx - 2)],
        dst_ref=cgot.at[pl.ds(0, 2 * n_gx - 2)],
        send_sem=zsend_sem.at[0],
        recv_sem=zrecv_sem.at[0],
        device_id=(lax.rem(gx + 1, n_gx), gy),
        device_id_type=MESH,
    )
    got_depth = pltpu.make_async_remote_copy(
        src_ref=dgot.at[pl.ds(0, n_gx - 1)],
        dst_ref=dgot.at[pl.ds(0, n_gx - 1)],
        send_sem=zsend_sem.at[1],
        recv_sem=zrecv_sem.at[1],
        device_id=(lax.rem(gx + 1, n_gx), gy),
        device_id_type=MESH,
    )
    own.wait()
    got.wait_recv()
    got_depth.wait_recv()
    frame[0:8, :] = jnp.zeros((8, NG), F32)
    frame[24:32, :] = jnp.zeros((8, NG), F32)
    for t in range(NT):
        holder = owner_ref[t]
        rank = jnp.int32(0)
        for t2 in range(t):
            rank = rank + jnp.where(owner_ref[t2] == holder, 1, 0)
        seen = cgot[2 * holder + rank].astype(F32)
        classes = dgot[holder]
        e = jnp.where(rank == 0, classes[0:1, :], classes[1:2, :])

        def pick(ref):
            out = jnp.full((1, 128), ref[0], F32)
            for value in range(1, 4):
                out = jnp.where(e == value, ref[value], out)
            return out

        level, lin, quad = pick(mean_ref), pick(one_ref), pick(two_ref)
        cell = smooth[:, TC * t : TC * t + TC]
        rate = level * jnp.exp(lin * cell + quad * cell * cell)
        frame[8:24, TC * t : TC * t + TC] = (seen - rate) * (lin + 2.0 * quad * cell)

    cols = []
    for b in range(3):
        inner = sum(stencil_ref[3 * a + b] * frame[9 - a : 25 - a, :] for a in range(3))
        outer = jnp.concatenate([stencil_ref[b] * frame[8:9, :], stencil_ref[6 + b] * frame[23:24, :]], 0)
        cols.append((inner, outer))
    pulled = roll(cols[0][0], NG - 1, 1) + cols[1][0] + roll(cols[2][0], 1, 1)
    pulled_edge = roll(cols[0][1], NG - 1, 1) + cols[1][1] + roll(cols[2][1], 1, 1)
    main, edge = field_rows(field)
    rows, halo = adjoint_rows(adjoints_of(pulled, main), adjoints_of(pulled_edge, edge), w, roll)
    for eb in range(4):
        cols = slice(128 * eb, 128 * eb + 128)
        nat[72 * eb : 72 * eb + 64, :] = rows[:, cols]
        outs = turn_list([nat[pl.ds(72 * eb + xl, 8, stride=8), :] for xl in range(8)], roll)
        for i in range(8):
            s3[128 * eb + 16 * i : 128 * eb + 16 * i + 8, :] = outs[i]
        s3[pl.ds(128 * eb + 8, 8, stride=16), :] = turn_vreg(halo[:, cols], roll)
    exchange(2, s3, r3, 16, 9)

    everything(2, r3, 9).wait_recv()
    mains = [
        jnp.concatenate([r3[pl.ds(2 * f + xh, 32, stride=16), :] for xh in range(2)], 0) for f in range(4)
    ]
    mains = halo_in(mains, r3[pl.ds(8, 32, stride=16), :], roll)
    modes = columns_forward(mains, cs, d8, tw)
    summed = flt[0] * modes[0] + flt[3] * modes[3] - sign * swap_parts(flt[1] * modes[1] + flt[2] * modes[2], roll)
    back = columns_inverse([summed], ct, d8, tw)[0]
    for xh in range(2):
        s4[pl.ds(xh, 32, stride=8), :] = back[32 * xh : 32 * xh + 32]
    exchange(3, s4, r4, 8, 2)

    everything(3, r4, 2).wait_recv()
    for xh in range(2):
        for eb in range(4):
            block = r4[pl.ds(64 * eb + xh, 8, stride=8), :]
            nat[72 * eb + 8 * xh : 72 * eb + 8 * xh + 8, :] = turn_vreg(block, roll)
    grad_ref[...] = rows_inverse(panels(nat, 0, 16), w) - noise_ref[...]

    for phase, (buf, count) in enumerate(((s1, 2), (s2, 9), (s3, 9), (s4, 2))):
        everything(phase, buf, count).wait_send()
    got.wait_send()
    got_depth.wait_send()


def local(tables, n_gx, n_gy, noise, stencil, mean_counts, bias_one, bias_two, owner, depth, counts):
    rows = noise.shape[1]
    slots = counts.shape[1]
    vmem = pl.BlockSpec(memory_space=pltpu.VMEM)
    smem = pl.BlockSpec(memory_space=pltpu.SMEM)
    out = jax.ShapeDtypeStruct((rows, NG), F32)
    grad, dens = pl.pallas_call(
        functools.partial(kernel, n_gx, n_gy),
        out_shape=(out, out),
        in_specs=[vmem] + [smem] * 5 + [vmem, pl.BlockSpec(memory_space=pl.ANY)] + [vmem] * 5,
        out_specs=(vmem, vmem),
        scratch_shapes=[
            pltpu.VMEM((256, 128), F32),
            pltpu.VMEM((256, 128), F32),
            pltpu.VMEM((512, 128), F32),
            pltpu.VMEM((512, 128), F32),
            pltpu.VMEM((512, 128), F32),
            pltpu.VMEM((512, 128), F32),
            pltpu.VMEM((256, 128), F32),
            pltpu.VMEM((256, 128), F32),
            pltpu.VMEM((288, 128), F32),
            pltpu.VMEM((96, NG), F32),
            pltpu.VMEM((32, NG), F32),
            pltpu.VMEM((n_gx, 8, 128), jnp.int32),
            pltpu.VMEM((n_gx, 8, 128), jnp.int32),
            pltpu.VMEM((slots, rows, TC), jnp.int32),
            pltpu.SemaphoreType.DMA((4,)),
            pltpu.SemaphoreType.DMA((4,)),
            pltpu.SemaphoreType.DMA((3,)),
            pltpu.SemaphoreType.DMA((2,)),
        ],
        compiler_params=pltpu.CompilerParams(collective_id=0, has_side_effects=True),
        name="posterior",
    )(
        noise.reshape(rows, NG),
        stencil,
        mean_counts,
        bias_one,
        bias_two,
        owner.reshape(-1),
        depth.reshape(slots, 1),
        counts.reshape(slots, rows, TC),
        *[jnp.asarray(table) for table in tables],
    )
    return grad[None], dens[None]


def solution(mesh):
    return jax.shard_map(
        functools.partial(local, make_tables(), mesh.shape["gx"], mesh.shape["gy"]),
        mesh=mesh,
        in_specs=(
            P("gx", "gy", None),
            P(),
            P(),
            P(),
            P(),
            P("gy", "gx", None, None),
            P("gx", None, "gy"),
            P("gx", None, "gy", None, None),
        ),
        out_specs=(P("gx", "gy", None), P("gx", "gy", None)),
        check_vma=False,
    )
```

```python
import functools
import math

import jax
import jax.numpy as jnp
import ml_dtypes
import numpy as np
from jax import lax
from jax.experimental import pallas as pl
from jax.experimental.pallas import tpu as pltpu
from jax.sharding import PartitionSpec as P

MESH = pl.DeviceIdType.MESH
NG = 512
TC = 128
NT = 4
AMPLITUDE = 0.75
GROWTH = 7.0 / 8.0
UNIT = 2.0 * math.pi / NG
F32 = jnp.float32
BF16 = jnp.bfloat16


def halves(table):
    high = table.astype(ml_dtypes.bfloat16)
    low = (table - high.astype(np.float64)).astype(ml_dtypes.bfloat16)
    return high, low


def make_tables():
    y = np.arange(256)[:, None]
    lane = np.arange(256)[None, :]
    half = 8 * (lane // 16) + lane % 8
    part = (lane // 8) % 2
    w = []
    for odd in (0, 1):
        turn = (y * (2 * half + odd)) % NG
        w.append(np.where(part == 0, np.cos(UNIT * turn), -np.sin(UNIT * turn)))
    w_tab = np.stack([piece for table in w for piece in halves(table)])
    k = np.arange(64)[:, None]
    row = np.arange(64)[None, :]
    turn = (k * (2 * (row % 32) + row // 32)) % 64
    cs = np.concatenate([np.cos(2 * math.pi * turn / 64), np.sin(2 * math.pi * turn / 64)], 0)
    hi, lo = halves(cs)
    cs_tab = np.concatenate([hi, lo, hi], 1)
    hi, lo = halves(np.concatenate([cs[:64].T, cs[64:].T], 1))
    ct_tab = np.concatenate([hi, lo, hi], 1)
    d8 = np.zeros((8, 2, 8, 8, 2, 8))
    for xl in range(8):
        for q in range(8):
            co, si = np.cos(2 * math.pi * (q * xl % 8) / 8), np.sin(2 * math.pi * (q * xl % 8) / 8)
            for m in range(8):
                d8[xl, 0, m, q, 0, m] = co
                d8[xl, 1, m, q, 0, m] = si
                d8[xl, 1, m, q, 1, m] = co
                d8[xl, 0, m, q, 1, m] = -si
    d8 = d8.reshape(128, 128)
    minus_i = np.zeros((128, 128))
    for g in range(8):
        for m in range(8):
            minus_i[g * 16 + 8 + m, g * 16 + m] = 1.0
            minus_i[g * 16 + m, g * 16 + 8 + m] = -1.0
    d8_tab = np.stack(halves(np.concatenate([d8, minus_i @ d8], 0)))
    kk = np.arange(64)[:, None]
    xl = (np.arange(128) // 16)[None, :]
    tw_tab = np.stack([np.cos(UNIT * kk * xl), np.sin(UNIT * kk * xl)]).astype(np.float32)
    return w_tab, cs_tab, ct_tab, d8_tab, tw_tab


def split(x):
    high = x.astype(BF16)
    return high, (x - high.astype(F32)).astype(BF16)


def nn(a, b):
    return lax.dot_general(a, b, (((1,), (0,)), ((), ())), preferred_element_type=F32)


def nt(a, b):
    return lax.dot_general(a, b, (((1,), (1,)), ((), ())), preferred_element_type=F32)


def dot3(mul, x, high, low):
    x_high, x_low = split(x)
    return mul(x_high, high) + (mul(x_high, low) + mul(x_low, high))


def left3(table, x):
    x_high, x_low = split(x)
    return nn(table, jnp.concatenate([x_high, x_high, x_low], 0))


def rows_forward(v, w):
    low, high = v[:, :256], v[:, 256:]
    return jnp.concatenate([dot3(nn, low + high, w[0], w[1]), dot3(nn, low - high, w[2], w[3])], 1)


def rows_inverse(s, w):
    even, odd = dot3(nt, s[:, :256], w[0], w[1]), dot3(nt, s[:, 256:], w[2], w[3])
    return jnp.concatenate([even + odd, even - odd], 1)


def columns_forward(fields, cs, d8, tw):
    turned = left3(cs, jnp.concatenate(fields, 1))
    tc, ts = tw
    parts = []
    for f in range(len(fields)):
        a, b = turned[:64, 128 * f : 128 * f + 128], turned[64:, 128 * f : 128 * f + 128]
        parts.append(jnp.concatenate([tc * a - ts * b, tc * b + ts * a], 1))
    out = dot3(nn, jnp.concatenate(parts, 0), d8[0], d8[1])
    return [out[64 * f : 64 * f + 64] for f in range(len(fields))]


def columns_inverse(fields, ct, d8, tw):
    out = dot3(nt, jnp.concatenate(fields, 0), d8[0], d8[1])
    tc, ts = tw
    parts = []
    for f in range(len(fields)):
        a, b = out[64 * f : 64 * f + 64, :128], out[64 * f : 64 * f + 64, 128:]
        parts.append(jnp.concatenate([tc * a + ts * b, tc * b - ts * a], 0))
    back = left3(ct, jnp.concatenate(parts, 1))
    return [back[:, 128 * f : 128 * f + 128] for f in range(len(fields))]


def swap_parts(v, roll):
    lane = lax.broadcasted_iota(jnp.int32, v.shape, 1)
    return jnp.where(lane // 8 % 2 == 0, roll(v, v.shape[1] - 8, 1), roll(v, 8, 1))


def part_sign(shape):
    lane = lax.broadcasted_iota(jnp.int32, shape, 1)
    return jnp.where(lane // 8 % 2 == 0, -1.0, 1.0).astype(F32)


def times_ky(v, roll):
    lane = lax.broadcasted_iota(jnp.int32, (1, NG), 1)
    e = lane // 16
    ky = UNIT * (2 * (8 * (e % 16) + lane % 8) + e // 16).astype(F32)
    return part_sign((1, NG)) * ky * swap_parts(v, roll)


def filters(e):
    shape = (64, 128)
    k = lax.broadcasted_iota(jnp.int32, shape, 0)
    lane = lax.broadcasted_iota(jnp.int32, shape, 1)
    mx = k + 64 * (lane // 16)
    my = 2 * (8 * (e % 16) + lane % 8) + e // 16
    kx = UNIT * jnp.where(mx > NG // 2, mx - NG, mx).astype(F32)
    ky = UNIT * my.astype(F32)
    k2 = kx * kx + ky * ky
    safe = jnp.where(k2 > 0, k2, 1.0)
    inverse_sq = jnp.where(k2 > 0, 1.0 / safe, 0.0)
    envelope = jnp.where(mx != NG // 2, AMPLITUDE * jnp.sqrt(k2) / (1.0 + k2), 0.0)
    weight = jnp.where(my == 0, 1.0, 2.0).astype(F32) / (NG * NG)
    base = weight * envelope
    return base, base * kx * inverse_sq, base * kx, base * inverse_sq


def turn_vreg(x, roll):
    row = lax.broadcasted_iota(jnp.int32, (8, 128), 0)
    group = lax.broadcasted_iota(jnp.int32, (8, 128), 1) // 16
    for s in (1, 2, 4):
        row_bit, group_bit = row // s % 2, group // s % 2
        down = roll(roll(x, 8 - s, 0), 16 * s, 1)
        up = down if s == 4 else roll(roll(x, s, 0), 128 - 16 * s, 1)
        x = jnp.where(row_bit == group_bit, x, jnp.where(row_bit == 0, down, up))
    return x


def turn_list(vs, roll):
    group = lax.broadcasted_iota(jnp.int32, vs[0].shape, 1) // 16
    vs = list(vs)
    for s in (1, 2, 4):
        low = group // s % 2 == 0
        for i in range(8):
            if i & s == 0:
                a, b = vs[i], vs[i + s]
                vs[i] = jnp.where(low, a, roll(b, 16 * s, 1))
                vs[i + s] = jnp.where(low, roll(a, 128 - 16 * s, 1), b)
    return vs


def panels(nat, start, stop):
    return jnp.concatenate([nat[72 * eb + start : 72 * eb + stop, :] for eb in range(4)], 1)


def halo_out(backs, roll):
    group = lax.broadcasted_iota(jnp.int32, (32, 128), 1) // 16
    before = after = jnp.zeros((32, 128), F32)
    for f, back in enumerate(backs):
        before = jnp.where(group == 2 * f, roll(back[32:], 16 * ((2 * f - 7) % 8), 1), before)
        shifted = roll(back[:32], 16 * (2 * f + 1), 1)
        after = jnp.where(group == 2 * f + 1, shifted, after)
    return jnp.where(group % 2 == 0, roll(before, 1, 0), roll(after, 31, 0))


def halo_in(mains, halo, roll):
    group = lax.broadcasted_iota(jnp.int32, (32, 128), 1) // 16
    from_next, from_prev = roll(halo, 31, 0), roll(halo, 1, 0)
    out = []
    for f, main in enumerate(mains):
        top = main[:32] + jnp.where(group == 0, roll(from_prev, 16 * ((8 - 2 * f - 1) % 8), 1), 0.0)
        end = main[32:] + jnp.where(group == 7, roll(from_next, 16 * (7 - 2 * f), 1), 0.0)
        out.append(jnp.concatenate([top, end], 0))
    return out


def spread(nat, halo, w, roll):
    rows = [nat[0:48], times_ky(nat[48:64], roll), times_ky(nat[0:16], roll), halo, times_ky(halo, roll)]
    return rows_inverse(jnp.concatenate(rows, 0), w)


def field_rows(out):
    main = (out[0:16], out[16:32], out[32:48], out[48:64], out[64:80])
    edge = (out[80:82], out[82:84], out[84:86], out[94:96], out[88:90])
    return main, edge


def density_of(fields):
    linear, shift_x, slope_x, shift_y, slope_y = fields
    return linear + GROWTH * linear * linear - (shift_x * slope_x + shift_y * slope_y)


def adjoints_of(pulled, fields):
    linear, shift_x, slope_x, shift_y, slope_y = fields
    return (
        pulled * (1.0 + 2.0 * GROWTH * linear),
        -pulled * slope_x,
        -pulled * shift_x,
        -pulled * slope_y,
        -pulled * shift_y,
    )


def adjoint_rows(main, edge, w, roll):
    none = jnp.zeros((2, NG), F32)
    rows = list(main) + [edge[0], edge[1], edge[2], none, edge[4], none, none, edge[3]]
    out = rows_forward(jnp.concatenate(rows, 0), w)
    nat = jnp.concatenate(
        [out[0:16] - times_ky(out[64:80], roll), out[16:48], -times_ky(out[48:64], roll)], 0
    )
    return nat, out[80:88] - times_ky(out[88:96], roll)


def far(i):
    return 8 + jnp.where(i % 2 == 0, i // 2, -(i + 1) // 2)


def plane_peers(gy):
    y, x, core = gy // 8, gy // 2 % 4, gy % 2
    steps = [(dy, dx, dc) for dy in range(4) for dx in range(4) for dc in range(2)][1:]
    steps.sort(key=lambda step: -(min(step[0], 4 - step[0]) + min(step[1], 4 - step[1])))
    return [(y + dy) % 4 * 8 + (x + dx) % 4 * 2 + (core + dc) % 2 for dy, dx, dc in steps]


def kernel(
    n_gx, n_gy, noise_hbm, stencil_hbm, mean_hbm, one_hbm, two_hbm, owner_hbm, depth_hbm, counts_ref,
    w_hbm, cs_hbm, ct_hbm, d8_hbm, tw_hbm, grad_ref, dens_ref,
    noise_ref, stencil_ref, mean_ref, one_ref, two_ref, owner_ref, depth_ref,
    w_ref, cs_ref, ct_ref, d8_ref, tw_ref, in_sem,
    s1, r1, s2, r2, s3, r3, s4, r4, nat, field, frame, dsend, dgot, cgot,
    send_sem, recv_sem, zsend_sem, zrecv_sem,
):
    roll = pltpu.roll
    gx, gy = lax.axis_index("gx"), lax.axis_index("gy")

    barrier = pltpu.get_barrier_semaphore()

    @pl.loop(0, n_gx - 1)
    def _(i):
        pl.semaphore_signal(barrier, inc=1, device_id=(lax.rem(gx + far(i), n_gx), gy), device_id_type=MESH)

    for to in plane_peers(gy):
        pl.semaphore_signal(barrier, inc=1, device_id=(gx, to), device_id_type=MESH)

    loads = [
        pltpu.make_async_copy(src, dst, in_sem.at[i])
        for i, (src, dst) in enumerate(
            (
                (noise_hbm, noise_ref), (w_hbm, w_ref), (depth_hbm, depth_ref), (cs_hbm, cs_ref), (ct_hbm, ct_ref),
                (d8_hbm, d8_ref), (tw_hbm, tw_ref), (stencil_hbm, stencil_ref), (mean_hbm, mean_ref),
                (one_hbm, one_ref), (two_hbm, two_ref), (owner_hbm, owner_ref),
            )
        )
    ]
    for load in loads:
        load.start()

    def exchange(phase, src, dst, pitch, count):
        for to in plane_peers(gy):
            pltpu.make_async_remote_copy(
                src_ref=src.at[pl.ds(pl.multiple_of(to * pitch, 8), count)],
                dst_ref=dst.at[pl.ds(pl.multiple_of(gy * pitch, 8), count)],
                send_sem=send_sem.at[phase],
                recv_sem=recv_sem.at[phase],
                device_id=(gx, to),
                device_id_type=MESH,
            ).start()

        mine = pl.ds(pl.multiple_of(gy * pitch, 8), pitch)
        dst[mine, :] = src[mine, :]

    def everything(phase, buf, count):
        rows = pl.ds(0, (n_gy - 1) * count)
        return pltpu.make_async_remote_copy(
            src_ref=buf.at[rows],
            dst_ref=buf.at[rows],
            send_sem=send_sem.at[phase],
            recv_sem=recv_sem.at[phase],
            device_id=(gx, lax.rem(gy + 1, n_gy)),
            device_id_type=MESH,
        )

    loads[0].wait()
    loads[1].wait()
    w = [w_ref[i] for i in range(4)]

    spec = rows_forward(noise_ref[...], w)
    for xh in range(2):
        for eb in range(4):
            block = spec[8 * xh : 8 * xh + 8, 128 * eb : 128 * eb + 128]
            s1[pl.ds(64 * eb + xh, 8, stride=8), :] = turn_vreg(block, roll)
    loads[2].wait()
    for slot in range(2 * n_gx):
        dsend[slot // 2, slot % 2 : slot % 2 + 1, :] = jnp.full((1, 128), depth_ref[slot], jnp.int32)

    pl.semaphore_wait(barrier, n_gy - 1 + n_gx - 1)
    exchange(0, s1, r1, 8, 2)

    @pl.loop(0, n_gx - 1)
    def _(i):
        to = lax.rem(gx + far(i), n_gx)
        pltpu.make_async_remote_copy(
            src_ref=counts_ref.at[pl.ds(2 * to, 2)],
            dst_ref=cgot.at[pl.ds(2 * gx, 2)],
            send_sem=zsend_sem.at[0],
            recv_sem=zrecv_sem.at[0],
            device_id=(to, gy),
            device_id_type=MESH,
        ).start()
        pltpu.make_async_remote_copy(
            src_ref=dsend.at[to, pl.ds(0, 2)],
            dst_ref=dgot.at[gx, pl.ds(0, 2)],
            send_sem=zsend_sem.at[1],
            recv_sem=zrecv_sem.at[1],
            device_id=(to, gy),
            device_id_type=MESH,
        ).start()

    own = pltpu.make_async_copy(counts_ref.at[pl.ds(2 * gx, 2)], cgot.at[pl.ds(2 * gx, 2)], zsend_sem.at[2])
    own.start()
    dgot[gx, 0:2, :] = dsend[gx, 0:2, :]

    flt = filters(gy)
    for load in loads[3:]:
        load.wait()
    tw = (tw_ref[0], tw_ref[1])
    d8 = (d8_ref[0], d8_ref[1])
    cs, ct = cs_ref[...], ct_ref[...]
    sign = part_sign((64, 128))

    everything(0, r1, 2).wait_recv()
    packed = jnp.concatenate([r1[pl.ds(xh, 32, stride=8), :] for xh in range(2)], 0)
    modes = columns_forward([packed], cs, d8, tw)[0]
    turned = sign * swap_parts(modes, roll)
    backs = columns_inverse([flt[0] * modes, flt[1] * turned, flt[2] * turned, flt[3] * modes], ct, d8, tw)
    for f in range(4):
        for xh in range(2):
            s2[pl.ds(2 * f + xh, 32, stride=16), :] = backs[f][32 * xh : 32 * xh + 32]
    s2[pl.ds(8, 32, stride=16), :] = halo_out(backs, roll)
    exchange(1, s2, r2, 16, 9)

    everything(1, r2, 9).wait_recv()
    for eb in range(4):
        outs = turn_list([r2[128 * eb + 16 * i : 128 * eb + 16 * i + 8, :] for i in range(8)], roll)
        for xl in range(8):
            nat[pl.ds(72 * eb + xl, 8, stride=8), :] = outs[xl]
        nat[72 * eb + 64 : 72 * eb + 72, :] = turn_vreg(r2[pl.ds(128 * eb + 8, 8, stride=16), :], roll)
    field[...] = spread(panels(nat, 0, 64), panels(nat, 64, 72), w, roll)
    main, edge = field_rows(field)
    dens = density_of(main)
    dens_edge = density_of(edge)
    dens_ref[...] = dens
    frame[8:24, :] = dens
    frame[7:8, :] = dens_edge[0:1]
    frame[24:25, :] = dens_edge[1:2]
    cols = []
    for b in range(3):
        cols.append(sum(stencil_ref[3 * a + b] * frame[7 + a : 23 + a, :] for a in range(3)))
    smooth = roll(cols[0], 1, 1) + cols[1] + roll(cols[2], NG - 1, 1)

    got = pltpu.make_async_remote_copy(
        src_ref=cgot.at[pl.ds(0, 2 * n_gx - 2)],
        dst_ref=cgot.at[pl.ds(0, 2 * n_gx - 2)],
        send_sem=zsend_sem.at[0],
        recv_sem=zrecv_sem.at[0],
        device_id=(lax.rem(gx + 1, n_gx), gy),
        device_id_type=MESH,
    )
    got_depth = pltpu.make_async_remote_copy(
        src_ref=dgot.at[pl.ds(0, n_gx - 1), pl.ds(0, 2)],
        dst_ref=dgot.at[pl.ds(0, n_gx - 1), pl.ds(0, 2)],
        send_sem=zsend_sem.at[1],
        recv_sem=zrecv_sem.at[1],
        device_id=(lax.rem(gx + 1, n_gx), gy),
        device_id_type=MESH,
    )
    own.wait()
    got.wait_recv()
    got_depth.wait_recv()
    frame[0:8, :] = jnp.zeros((8, NG), F32)
    frame[24:32, :] = jnp.zeros((8, NG), F32)
    for t in range(NT):
        holder = owner_ref[t]
        rank = jnp.int32(0)
        for t2 in range(t):
            rank = rank + jnp.where(owner_ref[t2] == holder, 1, 0)
        seen = cgot[2 * holder + rank].astype(F32)
        classes = dgot[holder]
        e = jnp.where(rank == 0, classes[0:1, :], classes[1:2, :])

        def pick(ref):
            out = jnp.full((1, 128), ref[0], F32)
            for value in range(1, 4):
                out = jnp.where(e == value, ref[value], out)
            return out

        level, lin, quad = pick(mean_ref), pick(one_ref), pick(two_ref)
        cell = smooth[:, TC * t : TC * t + TC]
        rate = level * jnp.exp(lin * cell + quad * cell * cell)
        frame[8:24, TC * t : TC * t + TC] = (seen - rate) * (lin + 2.0 * quad * cell)

    cols = []
    for b in range(3):
        inner = sum(stencil_ref[3 * a + b] * frame[9 - a : 25 - a, :] for a in range(3))
        outer = jnp.concatenate([stencil_ref[b] * frame[8:9, :], stencil_ref[6 + b] * frame[23:24, :]], 0)
        cols.append((inner, outer))
    pulled = roll(cols[0][0], NG - 1, 1) + cols[1][0] + roll(cols[2][0], 1, 1)
    pulled_edge = roll(cols[0][1], NG - 1, 1) + cols[1][1] + roll(cols[2][1], 1, 1)
    main, edge = field_rows(field)
    rows, halo = adjoint_rows(adjoints_of(pulled, main), adjoints_of(pulled_edge, edge), w, roll)
    for eb in range(4):
        cols = slice(128 * eb, 128 * eb + 128)
        nat[72 * eb : 72 * eb + 64, :] = rows[:, cols]
        outs = turn_list([nat[pl.ds(72 * eb + xl, 8, stride=8), :] for xl in range(8)], roll)
        for i in range(8):
            s3[128 * eb + 16 * i : 128 * eb + 16 * i + 8, :] = outs[i]
        s3[pl.ds(128 * eb + 8, 8, stride=16), :] = turn_vreg(halo[:, cols], roll)
    exchange(2, s3, r3, 16, 9)

    everything(2, r3, 9).wait_recv()
    mains = [
        jnp.concatenate([r3[pl.ds(2 * f + xh, 32, stride=16), :] for xh in range(2)], 0) for f in range(4)
    ]
    mains = halo_in(mains, r3[pl.ds(8, 32, stride=16), :], roll)
    modes = columns_forward(mains, cs, d8, tw)
    summed = flt[0] * modes[0] + flt[3] * modes[3] - sign * swap_parts(flt[1] * modes[1] + flt[2] * modes[2], roll)
    back = columns_inverse([summed], ct, d8, tw)[0]
    for xh in range(2):
        s4[pl.ds(xh, 32, stride=8), :] = back[32 * xh : 32 * xh + 32]
    exchange(3, s4, r4, 8, 2)

    everything(3, r4, 2).wait_recv()
    for xh in range(2):
        for eb in range(4):
            block = r4[pl.ds(64 * eb + xh, 8, stride=8), :]
            nat[72 * eb + 8 * xh : 72 * eb + 8 * xh + 8, :] = turn_vreg(block, roll)
    grad_ref[...] = rows_inverse(panels(nat, 0, 16), w) - noise_ref[...]

    for phase, (buf, count) in enumerate(((s1, 2), (s2, 9), (s3, 9), (s4, 2))):
        everything(phase, buf, count).wait_send()
    got.wait_send()
    got_depth.wait_send()


def local(tables, n_gx, n_gy, noise, stencil, mean_counts, bias_one, bias_two, owner, depth, counts):
    rows = noise.shape[1]
    slots = counts.shape[1]
    vmem = pl.BlockSpec(memory_space=pltpu.VMEM)
    out = jax.ShapeDtypeStruct((rows, NG), F32)
    grad, dens = pl.pallas_call(
        functools.partial(kernel, n_gx, n_gy),
        out_shape=(out, out),
        in_specs=[pl.BlockSpec(memory_space=pltpu.HBM)] * 13,
        out_specs=(vmem, vmem),
        scratch_shapes=[
            pltpu.VMEM((rows, NG), F32),
            pltpu.SMEM((9,), F32),
            pltpu.SMEM((4,), F32),
            pltpu.SMEM((4,), F32),
            pltpu.SMEM((4,), F32),
            pltpu.SMEM((NT,), jnp.int32),
            pltpu.SMEM((slots,), jnp.int32),
            *[pltpu.VMEM(table.shape, table.dtype) for table in tables],
            pltpu.SemaphoreType.DMA((12,)),
            pltpu.VMEM((256, 128), F32),
            pltpu.VMEM((256, 128), F32),
            pltpu.VMEM((512, 128), F32),
            pltpu.VMEM((512, 128), F32),
            pltpu.VMEM((512, 128), F32),
            pltpu.VMEM((512, 128), F32),
            pltpu.VMEM((256, 128), F32),
            pltpu.VMEM((256, 128), F32),
            pltpu.VMEM((288, 128), F32),
            pltpu.VMEM((96, NG), F32),
            pltpu.VMEM((32, NG), F32),
            pltpu.VMEM((n_gx, 8, 128), jnp.int32),
            pltpu.VMEM((n_gx, 8, 128), jnp.int32),
            pltpu.VMEM((slots, rows, TC), jnp.int32),
            pltpu.SemaphoreType.DMA((4,)),
            pltpu.SemaphoreType.DMA((4,)),
            pltpu.SemaphoreType.DMA((3,)),
            pltpu.SemaphoreType.DMA((2,)),
        ],
        compiler_params=pltpu.CompilerParams(collective_id=0, has_side_effects=True),
        name="posterior",
    )(
        noise.reshape(rows, NG),
        stencil,
        mean_counts,
        bias_one,
        bias_two,
        owner.reshape(-1),
        depth.reshape(slots),
        counts.reshape(slots, rows, TC),
        *[jnp.asarray(table) for table in tables],
    )
    return grad[None], dens[None]


def solution(mesh):
    return jax.shard_map(
        functools.partial(local, make_tables(), mesh.shape["gx"], mesh.shape["gy"]),
        mesh=mesh,
        in_specs=(
            P("gx", "gy", None),
            P(),
            P(),
            P(),
            P(),
            P("gy", "gx", None, None),
            P("gx", None, "gy"),
            P("gx", None, "gy", None, None),
        ),
        out_specs=(P("gx", "gy", None), P("gx", "gy", None)),
        check_vma=False,
    )
```

```python
import functools
import math

import jax
import jax.numpy as jnp
import ml_dtypes
import numpy as np
from jax import lax
from jax.experimental import pallas as pl
from jax.experimental.pallas import tpu as pltpu
from jax.sharding import PartitionSpec as P

MESH = pl.DeviceIdType.MESH
NG = 512
TC = 128
NT = 4
AMPLITUDE = 0.75
GROWTH = 7.0 / 8.0
UNIT = 2.0 * math.pi / NG
F32 = jnp.float32
BF16 = jnp.bfloat16


def halves(table):
    high = table.astype(ml_dtypes.bfloat16)
    low = (table - high.astype(np.float64)).astype(ml_dtypes.bfloat16)
    return high, low


def make_tables():
    y = np.arange(256)[:, None]
    lane = np.arange(256)[None, :]
    half = 8 * (lane // 16) + lane % 8
    part = (lane // 8) % 2
    w = []
    for odd in (0, 1):
        turn = (y * (2 * half + odd)) % NG
        w.append(np.where(part == 0, np.cos(UNIT * turn), -np.sin(UNIT * turn)))
    w_tab = np.stack([piece for table in w for piece in halves(table)])
    k = np.arange(64)[:, None]
    row = np.arange(64)[None, :]
    turn = (k * (2 * (row % 32) + row // 32)) % 64
    cs = np.concatenate([np.cos(2 * math.pi * turn / 64), np.sin(2 * math.pi * turn / 64)], 0)
    hi, lo = halves(cs)
    cs_tab = np.concatenate([hi, lo, hi], 1)
    hi, lo = halves(np.concatenate([cs[:64].T, cs[64:].T], 1))
    ct_tab = np.concatenate([hi, lo, hi], 1)
    d8 = np.zeros((8, 2, 8, 8, 2, 8))
    for xl in range(8):
        for q in range(8):
            co, si = np.cos(2 * math.pi * (q * xl % 8) / 8), np.sin(2 * math.pi * (q * xl % 8) / 8)
            for m in range(8):
                d8[xl, 0, m, q, 0, m] = co
                d8[xl, 1, m, q, 0, m] = si
                d8[xl, 1, m, q, 1, m] = co
                d8[xl, 0, m, q, 1, m] = -si
    d8 = d8.reshape(128, 128)
    minus_i = np.zeros((128, 128))
    for g in range(8):
        for m in range(8):
            minus_i[g * 16 + 8 + m, g * 16 + m] = 1.0
            minus_i[g * 16 + m, g * 16 + 8 + m] = -1.0
    d8_tab = np.stack(halves(np.concatenate([d8, minus_i @ d8], 0)))
    kk = np.arange(64)[:, None]
    xl = (np.arange(128) // 16)[None, :]
    tw_tab = np.stack([np.cos(UNIT * kk * xl), np.sin(UNIT * kk * xl)]).astype(np.float32)
    return w_tab, cs_tab, ct_tab, d8_tab, tw_tab


def split(x):
    high = x.astype(BF16)
    return high, (x - high.astype(F32)).astype(BF16)


def nn(a, b):
    return lax.dot_general(a, b, (((1,), (0,)), ((), ())), preferred_element_type=F32)


def nt(a, b):
    return lax.dot_general(a, b, (((1,), (1,)), ((), ())), preferred_element_type=F32)


def dot3(mul, x, high, low):
    x_high, x_low = split(x)
    return mul(x_high, high) + (mul(x_high, low) + mul(x_low, high))


def left3(table, x):
    x_high, x_low = split(x)
    return nn(table, jnp.concatenate([x_high, x_high, x_low], 0))


def rows_forward(v, w):
    low, high = v[:, :256], v[:, 256:]
    return jnp.concatenate([dot3(nn, low + high, w[0], w[1]), dot3(nn, low - high, w[2], w[3])], 1)


def rows_inverse(s, w):
    even, odd = dot3(nt, s[:, :256], w[0], w[1]), dot3(nt, s[:, 256:], w[2], w[3])
    return jnp.concatenate([even + odd, even - odd], 1)


def columns_forward(fields, cs, d8, tw):
    turned = left3(cs, jnp.concatenate(fields, 1))
    tc, ts = tw
    parts = []
    for f in range(len(fields)):
        a, b = turned[:64, 128 * f : 128 * f + 128], turned[64:, 128 * f : 128 * f + 128]
        parts.append(jnp.concatenate([tc * a - ts * b, tc * b + ts * a], 1))
    out = dot3(nn, jnp.concatenate(parts, 0), d8[0], d8[1])
    return [out[64 * f : 64 * f + 64] for f in range(len(fields))]


def columns_inverse(fields, ct, d8, tw):
    out = dot3(nt, jnp.concatenate(fields, 0), d8[0], d8[1])
    tc, ts = tw
    parts = []
    for f in range(len(fields)):
        a, b = out[64 * f : 64 * f + 64, :128], out[64 * f : 64 * f + 64, 128:]
        parts.append(jnp.concatenate([tc * a + ts * b, tc * b - ts * a], 0))
    back = left3(ct, jnp.concatenate(parts, 1))
    return [back[:, 128 * f : 128 * f + 128] for f in range(len(fields))]


def swap_parts(v, roll):
    lane = lax.broadcasted_iota(jnp.int32, v.shape, 1)
    return jnp.where(lane // 8 % 2 == 0, roll(v, v.shape[1] - 8, 1), roll(v, 8, 1))


def part_sign(shape):
    lane = lax.broadcasted_iota(jnp.int32, shape, 1)
    return jnp.where(lane // 8 % 2 == 0, -1.0, 1.0).astype(F32)


def times_ky(v, roll):
    lane = lax.broadcasted_iota(jnp.int32, (1, NG), 1)
    e = lane // 16
    ky = UNIT * (2 * (8 * (e % 16) + lane % 8) + e // 16).astype(F32)
    return part_sign((1, NG)) * ky * swap_parts(v, roll)


def filters(e):
    shape = (64, 128)
    k = lax.broadcasted_iota(jnp.int32, shape, 0)
    lane = lax.broadcasted_iota(jnp.int32, shape, 1)
    mx = k + 64 * (lane // 16)
    my = 2 * (8 * (e % 16) + lane % 8) + e // 16
    kx = UNIT * jnp.where(mx > NG // 2, mx - NG, mx).astype(F32)
    ky = UNIT * my.astype(F32)
    k2 = kx * kx + ky * ky
    safe = jnp.where(k2 > 0, k2, 1.0)
    inverse_sq = jnp.where(k2 > 0, 1.0 / safe, 0.0)
    envelope = jnp.where(mx != NG // 2, AMPLITUDE * jnp.sqrt(k2) / (1.0 + k2), 0.0)
    weight = jnp.where(my == 0, 1.0, 2.0).astype(F32) / (NG * NG)
    base = weight * envelope
    return base, base * kx * inverse_sq, base * kx, base * inverse_sq


def turn_vreg(x, roll):
    row = lax.broadcasted_iota(jnp.int32, (8, 128), 0)
    group = lax.broadcasted_iota(jnp.int32, (8, 128), 1) // 16
    for s in (1, 2, 4):
        row_bit, group_bit = row // s % 2, group // s % 2
        down = roll(roll(x, 8 - s, 0), 16 * s, 1)
        up = down if s == 4 else roll(roll(x, s, 0), 128 - 16 * s, 1)
        x = jnp.where(row_bit == group_bit, x, jnp.where(row_bit == 0, down, up))
    return x


def turn_list(vs, roll):
    group = lax.broadcasted_iota(jnp.int32, vs[0].shape, 1) // 16
    vs = list(vs)
    for s in (1, 2, 4):
        low = group // s % 2 == 0
        for i in range(8):
            if i & s == 0:
                a, b = vs[i], vs[i + s]
                vs[i] = jnp.where(low, a, roll(b, 16 * s, 1))
                vs[i + s] = jnp.where(low, roll(a, 128 - 16 * s, 1), b)
    return vs


def panels(nat, start, stop):
    return jnp.concatenate([nat[72 * eb + start : 72 * eb + stop, :] for eb in range(4)], 1)


def halo_out(backs, roll):
    group = lax.broadcasted_iota(jnp.int32, (32, 128), 1) // 16
    before = after = jnp.zeros((32, 128), F32)
    for f, back in enumerate(backs):
        before = jnp.where(group == 2 * f, roll(back[32:], 16 * ((2 * f - 7) % 8), 1), before)
        shifted = roll(back[:32], 16 * (2 * f + 1), 1)
        after = jnp.where(group == 2 * f + 1, shifted, after)
    return jnp.where(group % 2 == 0, roll(before, 1, 0), roll(after, 31, 0))


def halo_in(mains, halo, roll):
    group = lax.broadcasted_iota(jnp.int32, (32, 128), 1) // 16
    from_next, from_prev = roll(halo, 31, 0), roll(halo, 1, 0)
    out = []
    for f, main in enumerate(mains):
        top = main[:32] + jnp.where(group == 0, roll(from_prev, 16 * ((8 - 2 * f - 1) % 8), 1), 0.0)
        end = main[32:] + jnp.where(group == 7, roll(from_next, 16 * (7 - 2 * f), 1), 0.0)
        out.append(jnp.concatenate([top, end], 0))
    return out


def spread(nat, halo, w, roll):
    rows = [nat[0:48], times_ky(nat[48:64], roll), times_ky(nat[0:16], roll), halo, times_ky(halo, roll)]
    return rows_inverse(jnp.concatenate(rows, 0), w)


def field_rows(out):
    main = (out[0:16], out[16:32], out[32:48], out[48:64], out[64:80])
    edge = (out[80:82], out[82:84], out[84:86], out[94:96], out[88:90])
    return main, edge


def density_of(fields):
    linear, shift_x, slope_x, shift_y, slope_y = fields
    return linear + GROWTH * linear * linear - (shift_x * slope_x + shift_y * slope_y)


def adjoints_of(pulled, fields):
    linear, shift_x, slope_x, shift_y, slope_y = fields
    return (
        pulled * (1.0 + 2.0 * GROWTH * linear),
        -pulled * slope_x,
        -pulled * shift_x,
        -pulled * slope_y,
        -pulled * shift_y,
    )


def adjoint_rows(main, edge, w, roll):
    none = jnp.zeros((2, NG), F32)
    rows = list(main) + [edge[0], edge[1], edge[2], none, edge[4], none, none, edge[3]]
    out = rows_forward(jnp.concatenate(rows, 0), w)
    nat = jnp.concatenate(
        [out[0:16] - times_ky(out[64:80], roll), out[16:48], -times_ky(out[48:64], roll)], 0
    )
    return nat, out[80:88] - times_ky(out[88:96], roll)


def far(i):
    return 8 + jnp.where(i % 2 == 0, i // 2, -(i + 1) // 2)


def plane_peers(gy):
    y, x, core = gy // 8, gy // 2 % 4, gy % 2
    steps = [(dy, dx, dc) for dy in range(4) for dx in range(4) for dc in range(2)][1:]
    steps.sort(key=lambda step: -(min(step[0], 4 - step[0]) + min(step[1], 4 - step[1])))
    return [(y + dy) % 4 * 8 + (x + dx) % 4 * 2 + (core + dc) % 2 for dy, dx, dc in steps]


def kernel(
    n_gx, n_gy, noise_hbm, stencil_hbm, mean_hbm, one_hbm, two_hbm, owner_hbm, depth_hbm, counts_ref,
    w_hbm, cs_hbm, ct_hbm, d8_hbm, tw_hbm, out_ref,
    noise_ref, stencil_ref, mean_ref, one_ref, two_ref, owner_ref, depth_ref,
    w_ref, cs_ref, ct_ref, d8_ref, tw_ref, in_sem,
    s1, r1, s2, r2, s3, r3, s4, r4, nat, field, frame, dsend, dgot, cgot,
    send_sem, recv_sem, zsend_sem, zrecv_sem,
):
    roll = pltpu.roll
    gx, gy = lax.axis_index("gx"), lax.axis_index("gy")

    barrier = pltpu.get_barrier_semaphore()

    @pl.loop(0, n_gx - 1)
    def _(i):
        pl.semaphore_signal(barrier, inc=1, device_id=(lax.rem(gx + far(i), n_gx), gy), device_id_type=MESH)

    for to in plane_peers(gy):
        pl.semaphore_signal(barrier, inc=1, device_id=(gx, to), device_id_type=MESH)

    loads = [
        pltpu.make_async_copy(src, dst, in_sem.at[i])
        for i, (src, dst) in enumerate(
            (
                (noise_hbm, noise_ref), (w_hbm, w_ref), (depth_hbm, depth_ref), (cs_hbm, cs_ref), (ct_hbm, ct_ref),
                (d8_hbm, d8_ref), (tw_hbm, tw_ref), (stencil_hbm, stencil_ref), (mean_hbm, mean_ref),
                (one_hbm, one_ref), (two_hbm, two_ref), (owner_hbm, owner_ref),
            )
        )
    ]
    for load in loads:
        load.start()

    def exchange(phase, src, dst, pitch, count):
        for to in plane_peers(gy):
            pltpu.make_async_remote_copy(
                src_ref=src.at[pl.ds(pl.multiple_of(to * pitch, 8), count)],
                dst_ref=dst.at[pl.ds(pl.multiple_of(gy * pitch, 8), count)],
                send_sem=send_sem.at[phase],
                recv_sem=recv_sem.at[phase],
                device_id=(gx, to),
                device_id_type=MESH,
            ).start()

        mine = pl.ds(pl.multiple_of(gy * pitch, 8), pitch)
        dst[mine, :] = src[mine, :]

    def everything(phase, buf, count):
        rows = pl.ds(0, (n_gy - 1) * count)
        return pltpu.make_async_remote_copy(
            src_ref=buf.at[rows],
            dst_ref=buf.at[rows],
            send_sem=send_sem.at[phase],
            recv_sem=recv_sem.at[phase],
            device_id=(gx, lax.rem(gy + 1, n_gy)),
            device_id_type=MESH,
        )

    loads[0].wait()
    loads[1].wait()
    w = [w_ref[i] for i in range(4)]

    spec = rows_forward(noise_ref[...], w)
    for xh in range(2):
        for eb in range(4):
            block = spec[8 * xh : 8 * xh + 8, 128 * eb : 128 * eb + 128]
            s1[pl.ds(64 * eb + xh, 8, stride=8), :] = turn_vreg(block, roll)
    loads[2].wait()
    for slot in range(2 * n_gx):
        dsend[slot // 2, slot % 2 : slot % 2 + 1, :] = jnp.full((1, 128), depth_ref[slot], jnp.int32)

    pl.semaphore_wait(barrier, n_gy - 1 + n_gx - 1)
    exchange(0, s1, r1, 8, 2)

    @pl.loop(0, n_gx - 1)
    def _(i):
        to = lax.rem(gx + far(i), n_gx)
        pltpu.make_async_remote_copy(
            src_ref=counts_ref.at[pl.ds(2 * to, 2)],
            dst_ref=cgot.at[pl.ds(2 * gx, 2)],
            send_sem=zsend_sem.at[0],
            recv_sem=zrecv_sem.at[0],
            device_id=(to, gy),
            device_id_type=MESH,
        ).start()
        pltpu.make_async_remote_copy(
            src_ref=dsend.at[to, pl.ds(0, 2)],
            dst_ref=dgot.at[gx, pl.ds(0, 2)],
            send_sem=zsend_sem.at[1],
            recv_sem=zrecv_sem.at[1],
            device_id=(to, gy),
            device_id_type=MESH,
        ).start()

    own = pltpu.make_async_copy(counts_ref.at[pl.ds(2 * gx, 2)], cgot.at[pl.ds(2 * gx, 2)], zsend_sem.at[2])
    own.start()
    dgot[gx, 0:2, :] = dsend[gx, 0:2, :]

    flt = filters(gy)
    for load in loads[3:]:
        load.wait()
    tw = (tw_ref[0], tw_ref[1])
    d8 = (d8_ref[0], d8_ref[1])
    cs, ct = cs_ref[...], ct_ref[...]
    sign = part_sign((64, 128))

    everything(0, r1, 2).wait_recv()
    packed = jnp.concatenate([r1[pl.ds(xh, 32, stride=8), :] for xh in range(2)], 0)
    modes = columns_forward([packed], cs, d8, tw)[0]
    turned = sign * swap_parts(modes, roll)
    backs = columns_inverse([flt[0] * modes, flt[1] * turned, flt[2] * turned, flt[3] * modes], ct, d8, tw)
    for f in range(4):
        for xh in range(2):
            s2[pl.ds(2 * f + xh, 32, stride=16), :] = backs[f][32 * xh : 32 * xh + 32]
    s2[pl.ds(8, 32, stride=16), :] = halo_out(backs, roll)
    exchange(1, s2, r2, 16, 9)

    everything(1, r2, 9).wait_recv()
    for eb in range(4):
        outs = turn_list([r2[128 * eb + 16 * i : 128 * eb + 16 * i + 8, :] for i in range(8)], roll)
        for xl in range(8):
            nat[pl.ds(72 * eb + xl, 8, stride=8), :] = outs[xl]
        nat[72 * eb + 64 : 72 * eb + 72, :] = turn_vreg(r2[pl.ds(128 * eb + 8, 8, stride=16), :], roll)
    field[...] = spread(panels(nat, 0, 64), panels(nat, 64, 72), w, roll)
    main, edge = field_rows(field)
    dens = density_of(main)
    dens_edge = density_of(edge)
    out_ref[1] = dens
    frame[8:24, :] = dens
    frame[7:8, :] = dens_edge[0:1]
    frame[24:25, :] = dens_edge[1:2]
    cols = []
    for b in range(3):
        cols.append(sum(stencil_ref[3 * a + b] * frame[7 + a : 23 + a, :] for a in range(3)))
    smooth = roll(cols[0], 1, 1) + cols[1] + roll(cols[2], NG - 1, 1)

    got = pltpu.make_async_remote_copy(
        src_ref=cgot.at[pl.ds(0, 2 * n_gx - 2)],
        dst_ref=cgot.at[pl.ds(0, 2 * n_gx - 2)],
        send_sem=zsend_sem.at[0],
        recv_sem=zrecv_sem.at[0],
        device_id=(lax.rem(gx + 1, n_gx), gy),
        device_id_type=MESH,
    )
    got_depth = pltpu.make_async_remote_copy(
        src_ref=dgot.at[pl.ds(0, n_gx - 1), pl.ds(0, 2)],
        dst_ref=dgot.at[pl.ds(0, n_gx - 1), pl.ds(0, 2)],
        send_sem=zsend_sem.at[1],
        recv_sem=zrecv_sem.at[1],
        device_id=(lax.rem(gx + 1, n_gx), gy),
        device_id_type=MESH,
    )
    own.wait()
    got.wait_recv()
    got_depth.wait_recv()
    frame[0:8, :] = jnp.zeros((8, NG), F32)
    frame[24:32, :] = jnp.zeros((8, NG), F32)
    for t in range(NT):
        holder = owner_ref[t]
        rank = jnp.int32(0)
        for t2 in range(t):
            rank = rank + jnp.where(owner_ref[t2] == holder, 1, 0)
        seen = cgot[2 * holder + rank].astype(F32)
        classes = dgot[holder]
        e = jnp.where(rank == 0, classes[0:1, :], classes[1:2, :])

        def pick(ref):
            out = jnp.full((1, 128), ref[0], F32)
            for value in range(1, 4):
                out = jnp.where(e == value, ref[value], out)
            return out

        level, lin, quad = pick(mean_ref), pick(one_ref), pick(two_ref)
        cell = smooth[:, TC * t : TC * t + TC]
        rate = level * jnp.exp(lin * cell + quad * cell * cell)
        frame[8:24, TC * t : TC * t + TC] = (seen - rate) * (lin + 2.0 * quad * cell)

    cols = []
    for b in range(3):
        inner = sum(stencil_ref[3 * a + b] * frame[9 - a : 25 - a, :] for a in range(3))
        outer = jnp.concatenate([stencil_ref[b] * frame[8:9, :], stencil_ref[6 + b] * frame[23:24, :]], 0)
        cols.append((inner, outer))
    pulled = roll(cols[0][0], NG - 1, 1) + cols[1][0] + roll(cols[2][0], 1, 1)
    pulled_edge = roll(cols[0][1], NG - 1, 1) + cols[1][1] + roll(cols[2][1], 1, 1)
    main, edge = field_rows(field)
    rows, halo = adjoint_rows(adjoints_of(pulled, main), adjoints_of(pulled_edge, edge), w, roll)
    for eb in range(4):
        cols = slice(128 * eb, 128 * eb + 128)
        nat[72 * eb : 72 * eb + 64, :] = rows[:, cols]
        outs = turn_list([nat[pl.ds(72 * eb + xl, 8, stride=8), :] for xl in range(8)], roll)
        for i in range(8):
            s3[128 * eb + 16 * i : 128 * eb + 16 * i + 8, :] = outs[i]
        s3[pl.ds(128 * eb + 8, 8, stride=16), :] = turn_vreg(halo[:, cols], roll)
    exchange(2, s3, r3, 16, 9)

    everything(2, r3, 9).wait_recv()
    mains = [
        jnp.concatenate([r3[pl.ds(2 * f + xh, 32, stride=16), :] for xh in range(2)], 0) for f in range(4)
    ]
    mains = halo_in(mains, r3[pl.ds(8, 32, stride=16), :], roll)
    modes = columns_forward(mains, cs, d8, tw)
    summed = flt[0] * modes[0] + flt[3] * modes[3] - sign * swap_parts(flt[1] * modes[1] + flt[2] * modes[2], roll)
    back = columns_inverse([summed], ct, d8, tw)[0]
    for xh in range(2):
        s4[pl.ds(xh, 32, stride=8), :] = back[32 * xh : 32 * xh + 32]
    exchange(3, s4, r4, 8, 2)

    everything(3, r4, 2).wait_recv()
    for xh in range(2):
        for eb in range(4):
            block = r4[pl.ds(64 * eb + xh, 8, stride=8), :]
            nat[72 * eb + 8 * xh : 72 * eb + 8 * xh + 8, :] = turn_vreg(block, roll)
    out_ref[0] = rows_inverse(panels(nat, 0, 16), w) - noise_ref[...]

    for phase, (buf, count) in enumerate(((s1, 2), (s2, 9), (s3, 9), (s4, 2))):
        everything(phase, buf, count).wait_send()
    got.wait_send()
    got_depth.wait_send()


def local(tables, n_gx, n_gy, noise, stencil, mean_counts, bias_one, bias_two, owner, depth, counts):
    rows = noise.shape[1]
    slots = counts.shape[1]
    vmem = pl.BlockSpec(memory_space=pltpu.VMEM)
    both = pl.pallas_call(
        functools.partial(kernel, n_gx, n_gy),
        out_shape=jax.ShapeDtypeStruct((2, rows, NG), F32),
        in_specs=[pl.BlockSpec(memory_space=pltpu.HBM)] * 13,
        out_specs=pl.BlockSpec(memory_space=pltpu.VMEM),
        scratch_shapes=[
            pltpu.VMEM((rows, NG), F32),
            pltpu.SMEM((9,), F32),
            pltpu.SMEM((4,), F32),
            pltpu.SMEM((4,), F32),
            pltpu.SMEM((4,), F32),
            pltpu.SMEM((NT,), jnp.int32),
            pltpu.SMEM((slots,), jnp.int32),
            *[pltpu.VMEM(table.shape, table.dtype) for table in tables],
            pltpu.SemaphoreType.DMA((12,)),
            pltpu.VMEM((256, 128), F32),
            pltpu.VMEM((256, 128), F32),
            pltpu.VMEM((512, 128), F32),
            pltpu.VMEM((512, 128), F32),
            pltpu.VMEM((512, 128), F32),
            pltpu.VMEM((512, 128), F32),
            pltpu.VMEM((256, 128), F32),
            pltpu.VMEM((256, 128), F32),
            pltpu.VMEM((288, 128), F32),
            pltpu.VMEM((96, NG), F32),
            pltpu.VMEM((32, NG), F32),
            pltpu.VMEM((n_gx, 8, 128), jnp.int32),
            pltpu.VMEM((n_gx, 8, 128), jnp.int32),
            pltpu.VMEM((slots, rows, TC), jnp.int32),
            pltpu.SemaphoreType.DMA((4,)),
            pltpu.SemaphoreType.DMA((4,)),
            pltpu.SemaphoreType.DMA((3,)),
            pltpu.SemaphoreType.DMA((2,)),
        ],
        compiler_params=pltpu.CompilerParams(collective_id=0, has_side_effects=True, vmem_limit_bytes=16 * 1024 * 1024),
        name="posterior",
    )(
        *[
            pltpu.with_memory_space_constraint(x, pltpu.HBM)
            for x in (
                noise.reshape(rows, NG),
                stencil,
                mean_counts,
                bias_one,
                bias_two,
                owner.reshape(-1),
                depth.reshape(slots),
                counts.reshape(slots, rows, TC),
                *[jnp.asarray(table) for table in tables],
            )
        ],
    )
    return both[0:1], both[1:2]


def solution(mesh):
    return jax.shard_map(
        functools.partial(local, make_tables(), mesh.shape["gx"], mesh.shape["gy"]),
        mesh=mesh,
        in_specs=(
            P("gx", "gy", None),
            P(),
            P(),
            P(),
            P(),
            P("gy", "gx", None, None),
            P("gx", None, "gy"),
            P("gx", None, "gy", None, None),
        ),
        out_specs=(P("gx", "gy", None), P("gx", "gy", None)),
        check_vma=False,
    )
```

```python
import functools
import math

import jax
import jax.numpy as jnp
import ml_dtypes
import numpy as np
from jax import lax
from jax.experimental import pallas as pl
from jax.experimental.pallas import tpu as pltpu
from jax.sharding import PartitionSpec as P

MESH = pl.DeviceIdType.MESH
NG = 512
TC = 128
NT = 4
AMPLITUDE = 0.75
GROWTH = 7.0 / 8.0
UNIT = 2.0 * math.pi / NG
F32 = jnp.float32
BF16 = jnp.bfloat16


def halves(table):
    high = table.astype(ml_dtypes.bfloat16)
    low = (table - high.astype(np.float64)).astype(ml_dtypes.bfloat16)
    return high, low


def make_tables():
    y = np.arange(256)[:, None]
    lane = np.arange(256)[None, :]
    half = 8 * (lane // 16) + lane % 8
    part = (lane // 8) % 2
    w = []
    for odd in (0, 1):
        turn = (y * (2 * half + odd)) % NG
        w.append(np.where(part == 0, np.cos(UNIT * turn), -np.sin(UNIT * turn)))
    w_tab = np.stack([piece for table in w for piece in halves(table)])
    k = np.arange(64)[:, None]
    row = np.arange(64)[None, :]
    turn = (k * (2 * (row % 32) + row // 32)) % 64
    cs = np.concatenate([np.cos(2 * math.pi * turn / 64), np.sin(2 * math.pi * turn / 64)], 0)
    hi, lo = halves(cs)
    cs_tab = np.concatenate([hi, lo, hi], 1)
    hi, lo = halves(np.concatenate([cs[:64].T, cs[64:].T], 1))
    ct_tab = np.concatenate([hi, lo, hi], 1)
    d8 = np.zeros((8, 2, 8, 8, 2, 8))
    for xl in range(8):
        for q in range(8):
            co, si = np.cos(2 * math.pi * (q * xl % 8) / 8), np.sin(2 * math.pi * (q * xl % 8) / 8)
            for m in range(8):
                d8[xl, 0, m, q, 0, m] = co
                d8[xl, 1, m, q, 0, m] = si
                d8[xl, 1, m, q, 1, m] = co
                d8[xl, 0, m, q, 1, m] = -si
    d8 = d8.reshape(128, 128)
    minus_i = np.zeros((128, 128))
    for g in range(8):
        for m in range(8):
            minus_i[g * 16 + 8 + m, g * 16 + m] = 1.0
            minus_i[g * 16 + m, g * 16 + 8 + m] = -1.0
    d8_tab = np.stack(halves(np.concatenate([d8, minus_i @ d8], 0)))
    kk = np.arange(64)[:, None]
    xl = (np.arange(128) // 16)[None, :]
    tw_tab = np.stack([np.cos(UNIT * kk * xl), np.sin(UNIT * kk * xl)]).astype(np.float32)
    return w_tab, cs_tab, ct_tab, d8_tab, tw_tab


def split(x):
    high = x.astype(BF16)
    return high, (x - high.astype(F32)).astype(BF16)


def nn(a, b):
    return lax.dot_general(a, b, (((1,), (0,)), ((), ())), preferred_element_type=F32)


def nt(a, b):
    return lax.dot_general(a, b, (((1,), (1,)), ((), ())), preferred_element_type=F32)


def dot3(mul, x, high, low):
    x_high, x_low = split(x)
    return mul(x_high, high) + (mul(x_high, low) + mul(x_low, high))


def left3(table, x):
    x_high, x_low = split(x)
    return nn(table, jnp.concatenate([x_high, x_high, x_low], 0))


def rows_forward(v, w):
    low, high = v[:, :256], v[:, 256:]
    return jnp.concatenate([dot3(nn, low + high, w[0], w[1]), dot3(nn, low - high, w[2], w[3])], 1)


def rows_inverse(s, w):
    even, odd = dot3(nt, s[:, :256], w[0], w[1]), dot3(nt, s[:, 256:], w[2], w[3])
    return jnp.concatenate([even + odd, even - odd], 1)


def columns_forward(fields, cs, d8, tw):
    turned = left3(cs, jnp.concatenate(fields, 1))
    tc, ts = tw
    parts = []
    for f in range(len(fields)):
        a, b = turned[:64, 128 * f : 128 * f + 128], turned[64:, 128 * f : 128 * f + 128]
        parts.append(jnp.concatenate([tc * a - ts * b, tc * b + ts * a], 1))
    out = dot3(nn, jnp.concatenate(parts, 0), d8[0], d8[1])
    return [out[64 * f : 64 * f + 64] for f in range(len(fields))]


def columns_inverse(fields, ct, d8, tw):
    out = dot3(nt, jnp.concatenate(fields, 0), d8[0], d8[1])
    tc, ts = tw
    parts = []
    for f in range(len(fields)):
        a, b = out[64 * f : 64 * f + 64, :128], out[64 * f : 64 * f + 64, 128:]
        parts.append(jnp.concatenate([tc * a + ts * b, tc * b - ts * a], 0))
    back = left3(ct, jnp.concatenate(parts, 1))
    return [back[:, 128 * f : 128 * f + 128] for f in range(len(fields))]


def swap_parts(v, roll):
    lane = lax.broadcasted_iota(jnp.int32, v.shape, 1)
    return jnp.where(lane // 8 % 2 == 0, roll(v, v.shape[1] - 8, 1), roll(v, 8, 1))


def part_sign(shape):
    lane = lax.broadcasted_iota(jnp.int32, shape, 1)
    return jnp.where(lane // 8 % 2 == 0, -1.0, 1.0).astype(F32)


def times_ky(v, roll):
    lane = lax.broadcasted_iota(jnp.int32, (1, NG), 1)
    e = lane // 16
    ky = UNIT * (2 * (8 * (e % 16) + lane % 8) + e // 16).astype(F32)
    return part_sign((1, NG)) * ky * swap_parts(v, roll)


def filters(e):
    shape = (64, 128)
    k = lax.broadcasted_iota(jnp.int32, shape, 0)
    lane = lax.broadcasted_iota(jnp.int32, shape, 1)
    mx = k + 64 * (lane // 16)
    my = 2 * (8 * (e % 16) + lane % 8) + e // 16
    kx = UNIT * jnp.where(mx > NG // 2, mx - NG, mx).astype(F32)
    ky = UNIT * my.astype(F32)
    k2 = kx * kx + ky * ky
    safe = jnp.where(k2 > 0, k2, 1.0)
    inverse_sq = jnp.where(k2 > 0, 1.0 / safe, 0.0)
    envelope = jnp.where(mx != NG // 2, AMPLITUDE * jnp.sqrt(k2) / (1.0 + k2), 0.0)
    weight = jnp.where(my == 0, 1.0, 2.0).astype(F32) / (NG * NG)
    base = weight * envelope
    return base, base * kx * inverse_sq, base * kx, base * inverse_sq


def turn_vreg(x, roll):
    row = lax.broadcasted_iota(jnp.int32, (8, 128), 0)
    group = lax.broadcasted_iota(jnp.int32, (8, 128), 1) // 16
    for s in (1, 2, 4):
        row_bit, group_bit = row // s % 2, group // s % 2
        down = roll(roll(x, 8 - s, 0), 16 * s, 1)
        up = down if s == 4 else roll(roll(x, s, 0), 128 - 16 * s, 1)
        x = jnp.where(row_bit == group_bit, x, jnp.where(row_bit == 0, down, up))
    return x


def turn_list(vs, roll):
    group = lax.broadcasted_iota(jnp.int32, vs[0].shape, 1) // 16
    vs = list(vs)
    for s in (1, 2, 4):
        low = group // s % 2 == 0
        for i in range(8):
            if i & s == 0:
                a, b = vs[i], vs[i + s]
                vs[i] = jnp.where(low, a, roll(b, 16 * s, 1))
                vs[i + s] = jnp.where(low, roll(a, 128 - 16 * s, 1), b)
    return vs


def panels(nat, start, stop):
    return jnp.concatenate([nat[72 * eb + start : 72 * eb + stop, :] for eb in range(4)], 1)


def halo_out(backs, roll):
    group = lax.broadcasted_iota(jnp.int32, (32, 128), 1) // 16
    before = after = jnp.zeros((32, 128), F32)
    for f, back in enumerate(backs):
        before = jnp.where(group == 2 * f, roll(back[32:], 16 * ((2 * f - 7) % 8), 1), before)
        shifted = roll(back[:32], 16 * (2 * f + 1), 1)
        after = jnp.where(group == 2 * f + 1, shifted, after)
    return jnp.where(group % 2 == 0, roll(before, 1, 0), roll(after, 31, 0))


def halo_in(mains, halo, roll):
    group = lax.broadcasted_iota(jnp.int32, (32, 128), 1) // 16
    from_next, from_prev = roll(halo, 31, 0), roll(halo, 1, 0)
    out = []
    for f, main in enumerate(mains):
        top = main[:32] + jnp.where(group == 0, roll(from_prev, 16 * ((8 - 2 * f - 1) % 8), 1), 0.0)
        end = main[32:] + jnp.where(group == 7, roll(from_next, 16 * (7 - 2 * f), 1), 0.0)
        out.append(jnp.concatenate([top, end], 0))
    return out


def spread(nat, halo, w, roll):
    rows = [nat[0:48], times_ky(nat[48:64], roll), times_ky(nat[0:16], roll), halo, times_ky(halo, roll)]
    return rows_inverse(jnp.concatenate(rows, 0), w)


def field_rows(out):
    main = (out[0:16], out[16:32], out[32:48], out[48:64], out[64:80])
    edge = (out[80:82], out[82:84], out[84:86], out[94:96], out[88:90])
    return main, edge


def density_of(fields):
    linear, shift_x, slope_x, shift_y, slope_y = fields
    return linear + GROWTH * linear * linear - (shift_x * slope_x + shift_y * slope_y)


def adjoints_of(pulled, fields):
    linear, shift_x, slope_x, shift_y, slope_y = fields
    return (
        pulled * (1.0 + 2.0 * GROWTH * linear),
        -pulled * slope_x,
        -pulled * shift_x,
        -pulled * slope_y,
        -pulled * shift_y,
    )


def adjoint_rows(main, edge, w, roll):
    none = jnp.zeros((2, NG), F32)
    rows = list(main) + [edge[0], edge[1], edge[2], none, edge[4], none, none, edge[3]]
    out = rows_forward(jnp.concatenate(rows, 0), w)
    nat = jnp.concatenate(
        [out[0:16] - times_ky(out[64:80], roll), out[16:48], -times_ky(out[48:64], roll)], 0
    )
    return nat, out[80:88] - times_ky(out[88:96], roll)


def far(i):
    return 8 + jnp.where(i % 2 == 0, i // 2, -(i + 1) // 2)


def plane_peers(gy):
    y, x, core = gy // 8, gy // 2 % 4, gy % 2
    steps = [(dy, dx, dc) for dy in range(4) for dx in range(4) for dc in range(2)][1:]
    steps.sort(key=lambda step: -(min(step[0], 4 - step[0]) + min(step[1], 4 - step[1])))
    return [(y + dy) % 4 * 8 + (x + dx) % 4 * 2 + (core + dc) % 2 for dy, dx, dc in steps]


def kernel(
    n_gx, n_gy, noise_hbm, stencil_hbm, mean_hbm, one_hbm, two_hbm, owner_hbm, depth_hbm, counts_ref,
    w_hbm, cs_hbm, ct_hbm, d8_hbm, tw_hbm, out_ref,
    noise_ref, stencil_ref, mean_ref, one_ref, two_ref, owner_ref, depth_ref,
    w_ref, cs_ref, ct_ref, d8_ref, tw_ref, in_sem,
    s1, r1, s2, r2, s3, r3, s4, r4, nat, field, frame, dsend, dgot, cgot,
    send_sem, recv_sem, zsend_sem, zrecv_sem,
):
    roll = pltpu.roll
    gx, gy = lax.axis_index("gx"), lax.axis_index("gy")

    barrier = pltpu.get_barrier_semaphore()

    @pl.loop(0, n_gx - 1)
    def _(i):
        pl.semaphore_signal(barrier, inc=1, device_id=(lax.rem(gx + far(i), n_gx), gy), device_id_type=MESH)

    for to in plane_peers(gy):
        pl.semaphore_signal(barrier, inc=1, device_id=(gx, to), device_id_type=MESH)

    loads = [
        pltpu.make_async_copy(src, dst, in_sem.at[i])
        for i, (src, dst) in enumerate(
            (
                (noise_hbm, noise_ref), (w_hbm, w_ref), (depth_hbm, depth_ref), (cs_hbm, cs_ref), (ct_hbm, ct_ref),
                (d8_hbm, d8_ref), (tw_hbm, tw_ref), (stencil_hbm, stencil_ref), (mean_hbm, mean_ref),
                (one_hbm, one_ref), (two_hbm, two_ref), (owner_hbm, owner_ref),
            )
        )
    ]
    for load in loads:
        load.start()

    def exchange(phase, src, dst, pitch, count):
        for to in plane_peers(gy):
            pltpu.make_async_remote_copy(
                src_ref=src.at[pl.ds(pl.multiple_of(to * pitch, 8), count)],
                dst_ref=dst.at[pl.ds(pl.multiple_of(gy * pitch, 8), count)],
                send_sem=send_sem.at[phase],
                recv_sem=recv_sem.at[phase],
                device_id=(gx, to),
                device_id_type=MESH,
            ).start()

        mine = pl.ds(pl.multiple_of(gy * pitch, 8), pitch)
        dst[mine, :] = src[mine, :]

    def everything(phase, buf, count):
        rows = pl.ds(0, (n_gy - 1) * count)
        return pltpu.make_async_remote_copy(
            src_ref=buf.at[rows],
            dst_ref=buf.at[rows],
            send_sem=send_sem.at[phase],
            recv_sem=recv_sem.at[phase],
            device_id=(gx, lax.rem(gy + 1, n_gy)),
            device_id_type=MESH,
        )

    loads[0].wait()
    loads[1].wait()
    w = [w_ref[i] for i in range(4)]

    spec = rows_forward(noise_ref[...], w)
    for xh in range(2):
        for eb in range(4):
            block = spec[8 * xh : 8 * xh + 8, 128 * eb : 128 * eb + 128]
            s1[pl.ds(64 * eb + xh, 8, stride=8), :] = turn_vreg(block, roll)
    loads[2].wait()
    left = lax.broadcasted_iota(jnp.int32, (1, 128), 1) < 64
    for other in range(n_gx):
        dsend[other, 0:1, :] = jnp.where(left, depth_ref[2 * other], depth_ref[2 * other + 1])

    pl.semaphore_wait(barrier, n_gy - 1 + n_gx - 1)

    @pl.loop(0, n_gx - 1)
    def _(i):
        to = lax.rem(gx + far(i), n_gx)
        pltpu.make_async_remote_copy(
            src_ref=counts_ref.at[pl.ds(2 * to, 2)],
            dst_ref=cgot.at[pl.ds(2 * gx, 2)],
            send_sem=zsend_sem.at[0],
            recv_sem=zrecv_sem.at[0],
            device_id=(to, gy),
            device_id_type=MESH,
        ).start()

    exchange(0, s1, r1, 8, 2)

    @pl.loop(0, n_gx - 1)
    def _(i):
        to = lax.rem(gx + far(i), n_gx)
        pltpu.make_async_remote_copy(
            src_ref=dsend.at[to, pl.ds(0, 1)],
            dst_ref=dgot.at[gx, pl.ds(0, 1)],
            send_sem=zsend_sem.at[1],
            recv_sem=zrecv_sem.at[1],
            device_id=(to, gy),
            device_id_type=MESH,
        ).start()

    own = pltpu.make_async_copy(counts_ref.at[pl.ds(2 * gx, 2)], cgot.at[pl.ds(2 * gx, 2)], zsend_sem.at[2])
    own.start()
    dgot[gx, 0:1, :] = dsend[gx, 0:1, :]

    flt = filters(gy)
    for load in loads[3:]:
        load.wait()
    tw = (tw_ref[0], tw_ref[1])
    d8 = (d8_ref[0], d8_ref[1])
    cs, ct = cs_ref[...], ct_ref[...]
    sign = part_sign((64, 128))

    everything(0, r1, 2).wait_recv()
    packed = jnp.concatenate([r1[pl.ds(xh, 32, stride=8), :] for xh in range(2)], 0)
    modes = columns_forward([packed], cs, d8, tw)[0]
    turned = sign * swap_parts(modes, roll)
    backs = columns_inverse([flt[0] * modes, flt[1] * turned, flt[2] * turned, flt[3] * modes], ct, d8, tw)
    for f in range(4):
        for xh in range(2):
            s2[pl.ds(2 * f + xh, 32, stride=16), :] = backs[f][32 * xh : 32 * xh + 32]
    s2[pl.ds(8, 32, stride=16), :] = halo_out(backs, roll)
    exchange(1, s2, r2, 16, 9)

    everything(1, r2, 9).wait_recv()
    for eb in range(4):
        outs = turn_list([r2[128 * eb + 16 * i : 128 * eb + 16 * i + 8, :] for i in range(8)], roll)
        for xl in range(8):
            nat[pl.ds(72 * eb + xl, 8, stride=8), :] = outs[xl]
        nat[72 * eb + 64 : 72 * eb + 72, :] = turn_vreg(r2[pl.ds(128 * eb + 8, 8, stride=16), :], roll)
    field[...] = spread(panels(nat, 0, 64), panels(nat, 64, 72), w, roll)
    main, edge = field_rows(field)
    dens = density_of(main)
    dens_edge = density_of(edge)
    out_ref[1] = dens
    frame[8:24, :] = dens
    frame[7:8, :] = dens_edge[0:1]
    frame[24:25, :] = dens_edge[1:2]
    cols = []
    for b in range(3):
        cols.append(sum(stencil_ref[3 * a + b] * frame[7 + a : 23 + a, :] for a in range(3)))
    smooth = roll(cols[0], 1, 1) + cols[1] + roll(cols[2], NG - 1, 1)

    got = pltpu.make_async_remote_copy(
        src_ref=cgot.at[pl.ds(0, 2 * n_gx - 2)],
        dst_ref=cgot.at[pl.ds(0, 2 * n_gx - 2)],
        send_sem=zsend_sem.at[0],
        recv_sem=zrecv_sem.at[0],
        device_id=(lax.rem(gx + 1, n_gx), gy),
        device_id_type=MESH,
    )
    got_depth = pltpu.make_async_remote_copy(
        src_ref=dgot.at[pl.ds(0, n_gx - 1), pl.ds(0, 1)],
        dst_ref=dgot.at[pl.ds(0, n_gx - 1), pl.ds(0, 1)],
        send_sem=zsend_sem.at[1],
        recv_sem=zrecv_sem.at[1],
        device_id=(lax.rem(gx + 1, n_gx), gy),
        device_id_type=MESH,
    )
    own.wait()
    got.wait_recv()
    got_depth.wait_recv()
    frame[0:8, :] = jnp.zeros((8, NG), F32)
    frame[24:32, :] = jnp.zeros((8, NG), F32)
    for t in range(NT):
        holder = owner_ref[t]
        rank = jnp.int32(0)
        for t2 in range(t):
            rank = rank + jnp.where(owner_ref[t2] == holder, 1, 0)
        seen = cgot[2 * holder + rank].astype(F32)
        classes = dgot[holder]
        row, turned_row = classes[0:1, :], roll(classes, 64, 1)[0:1, :]
        first, second = jnp.where(left, row, turned_row), jnp.where(left, turned_row, row)
        e = jnp.where(rank == 0, first, second)

        def pick(ref):
            out = jnp.full((1, 128), ref[0], F32)
            for value in range(1, 4):
                out = jnp.where(e == value, ref[value], out)
            return out

        level, lin, quad = pick(mean_ref), pick(one_ref), pick(two_ref)
        cell = smooth[:, TC * t : TC * t + TC]
        rate = level * jnp.exp(lin * cell + quad * cell * cell)
        frame[8:24, TC * t : TC * t + TC] = (seen - rate) * (lin + 2.0 * quad * cell)

    cols = []
    for b in range(3):
        inner = sum(stencil_ref[3 * a + b] * frame[9 - a : 25 - a, :] for a in range(3))
        outer = jnp.concatenate([stencil_ref[b] * frame[8:9, :], stencil_ref[6 + b] * frame[23:24, :]], 0)
        cols.append((inner, outer))
    pulled = roll(cols[0][0], NG - 1, 1) + cols[1][0] + roll(cols[2][0], 1, 1)
    pulled_edge = roll(cols[0][1], NG - 1, 1) + cols[1][1] + roll(cols[2][1], 1, 1)
    main, edge = field_rows(field)
    rows, halo = adjoint_rows(adjoints_of(pulled, main), adjoints_of(pulled_edge, edge), w, roll)
    for eb in range(4):
        cols = slice(128 * eb, 128 * eb + 128)
        nat[72 * eb : 72 * eb + 64, :] = rows[:, cols]
        outs = turn_list([nat[pl.ds(72 * eb + xl, 8, stride=8), :] for xl in range(8)], roll)
        for i in range(8):
            s3[128 * eb + 16 * i : 128 * eb + 16 * i + 8, :] = outs[i]
        s3[pl.ds(128 * eb + 8, 8, stride=16), :] = turn_vreg(halo[:, cols], roll)
    exchange(2, s3, r3, 16, 9)

    everything(2, r3, 9).wait_recv()
    mains = [
        jnp.concatenate([r3[pl.ds(2 * f + xh, 32, stride=16), :] for xh in range(2)], 0) for f in range(4)
    ]
    mains = halo_in(mains, r3[pl.ds(8, 32, stride=16), :], roll)
    modes = columns_forward(mains, cs, d8, tw)
    summed = flt[0] * modes[0] + flt[3] * modes[3] - sign * swap_parts(flt[1] * modes[1] + flt[2] * modes[2], roll)
    back = columns_inverse([summed], ct, d8, tw)[0]
    for xh in range(2):
        s4[pl.ds(xh, 32, stride=8), :] = back[32 * xh : 32 * xh + 32]
    exchange(3, s4, r4, 8, 2)

    everything(3, r4, 2).wait_recv()
    for xh in range(2):
        for eb in range(4):
            block = r4[pl.ds(64 * eb + xh, 8, stride=8), :]
            nat[72 * eb + 8 * xh : 72 * eb + 8 * xh + 8, :] = turn_vreg(block, roll)
    out_ref[0] = rows_inverse(panels(nat, 0, 16), w) - noise_ref[...]

    for phase, (buf, count) in enumerate(((s1, 2), (s2, 9), (s3, 9), (s4, 2))):
        everything(phase, buf, count).wait_send()
    got.wait_send()
    got_depth.wait_send()


def local(tables, n_gx, n_gy, noise, stencil, mean_counts, bias_one, bias_two, owner, depth, counts):
    rows = noise.shape[1]
    slots = counts.shape[1]
    vmem = pl.BlockSpec(memory_space=pltpu.VMEM)
    both = pl.pallas_call(
        functools.partial(kernel, n_gx, n_gy),
        out_shape=jax.ShapeDtypeStruct((2, rows, NG), F32),
        in_specs=[pl.BlockSpec(memory_space=pltpu.HBM)] * 13,
        out_specs=pl.BlockSpec(memory_space=pltpu.VMEM),
        scratch_shapes=[
            pltpu.VMEM((rows, NG), F32),
            pltpu.SMEM((9,), F32),
            pltpu.SMEM((4,), F32),
            pltpu.SMEM((4,), F32),
            pltpu.SMEM((4,), F32),
            pltpu.SMEM((NT,), jnp.int32),
            pltpu.SMEM((slots,), jnp.int32),
            *[pltpu.VMEM(table.shape, table.dtype) for table in tables],
            pltpu.SemaphoreType.DMA((12,)),
            pltpu.VMEM((256, 128), F32),
            pltpu.VMEM((256, 128), F32),
            pltpu.VMEM((512, 128), F32),
            pltpu.VMEM((512, 128), F32),
            pltpu.VMEM((512, 128), F32),
            pltpu.VMEM((512, 128), F32),
            pltpu.VMEM((256, 128), F32),
            pltpu.VMEM((256, 128), F32),
            pltpu.VMEM((288, 128), F32),
            pltpu.VMEM((96, NG), F32),
            pltpu.VMEM((32, NG), F32),
            pltpu.VMEM((n_gx, 8, 128), jnp.int32),
            pltpu.VMEM((n_gx, 8, 128), jnp.int32),
            pltpu.VMEM((slots, rows, TC), jnp.int32),
            pltpu.SemaphoreType.DMA((4,)),
            pltpu.SemaphoreType.DMA((4,)),
            pltpu.SemaphoreType.DMA((3,)),
            pltpu.SemaphoreType.DMA((2,)),
        ],
        compiler_params=pltpu.CompilerParams(collective_id=0, has_side_effects=True, vmem_limit_bytes=16 * 1024 * 1024),
        name="posterior",
    )(
        *[
            pltpu.with_memory_space_constraint(x, pltpu.HBM)
            for x in (
                noise.reshape(rows, NG),
                stencil,
                mean_counts,
                bias_one,
                bias_two,
                owner.reshape(-1),
                depth.reshape(slots),
                counts.reshape(slots, rows, TC),
                *[jnp.asarray(table) for table in tables],
            )
        ],
    )
    return both[0:1], both[1:2]


def solution(mesh):
    return jax.shard_map(
        functools.partial(local, make_tables(), mesh.shape["gx"], mesh.shape["gy"]),
        mesh=mesh,
        in_specs=(
            P("gx", "gy", None),
            P(),
            P(),
            P(),
            P(),
            P("gy", "gx", None, None),
            P("gx", None, "gy"),
            P("gx", None, "gy", None, None),
        ),
        out_specs=(P("gx", "gy", None), P("gx", "gy", None)),
        check_vma=False,
    )
```

```python
import functools
import math

import jax
import jax.numpy as jnp
import ml_dtypes
import numpy as np
from jax import lax
from jax.experimental import pallas as pl
from jax.experimental.pallas import tpu as pltpu
from jax.sharding import PartitionSpec as P

MESH = pl.DeviceIdType.MESH
NG = 512
TC = 128
NT = 4
AMPLITUDE = 0.75
GROWTH = 7.0 / 8.0
UNIT = 2.0 * math.pi / NG
F32 = jnp.float32
BF16 = jnp.bfloat16


def halves(table):
    high = table.astype(ml_dtypes.bfloat16)
    low = (table - high.astype(np.float64)).astype(ml_dtypes.bfloat16)
    return high, low


def make_tables():
    y = np.arange(256)[:, None]
    lane = np.arange(256)[None, :]
    half = 8 * (lane // 16) + lane % 8
    part = (lane // 8) % 2
    w = []
    for odd in (0, 1):
        turn = (y * (2 * half + odd)) % NG
        w.append(np.where(part == 0, np.cos(UNIT * turn), -np.sin(UNIT * turn)))
    w_tab = np.stack([piece for table in w for piece in halves(table)])
    k = np.arange(64)[:, None]
    row = np.arange(64)[None, :]
    turn = (k * (2 * (row % 32) + row // 32)) % 64
    cs = np.concatenate([np.cos(2 * math.pi * turn / 64), np.sin(2 * math.pi * turn / 64)], 0)
    hi, lo = halves(cs)
    cs_tab = np.concatenate([hi, lo, hi], 1)
    hi, lo = halves(np.concatenate([cs[:64].T, cs[64:].T], 1))
    ct_tab = np.concatenate([hi, lo, hi], 1)
    d8 = np.zeros((8, 2, 8, 8, 2, 8))
    for xl in range(8):
        for q in range(8):
            co, si = np.cos(2 * math.pi * (q * xl % 8) / 8), np.sin(2 * math.pi * (q * xl % 8) / 8)
            for m in range(8):
                d8[xl, 0, m, q, 0, m] = co
                d8[xl, 1, m, q, 0, m] = si
                d8[xl, 1, m, q, 1, m] = co
                d8[xl, 0, m, q, 1, m] = -si
    d8 = d8.reshape(128, 128)
    minus_i = np.zeros((128, 128))
    for g in range(8):
        for m in range(8):
            minus_i[g * 16 + 8 + m, g * 16 + m] = 1.0
            minus_i[g * 16 + m, g * 16 + 8 + m] = -1.0
    d8_tab = np.stack(halves(np.concatenate([d8, minus_i @ d8], 0)))
    kk = np.arange(64)[:, None]
    xl = (np.arange(128) // 16)[None, :]
    tw_tab = np.stack([np.cos(UNIT * kk * xl), np.sin(UNIT * kk * xl)]).astype(np.float32)
    return w_tab, cs_tab, ct_tab, d8_tab, tw_tab


def split(x):
    high = x.astype(BF16)
    return high, (x - high.astype(F32)).astype(BF16)


def nn(a, b):
    return lax.dot_general(a, b, (((1,), (0,)), ((), ())), preferred_element_type=F32)


def nt(a, b):
    return lax.dot_general(a, b, (((1,), (1,)), ((), ())), preferred_element_type=F32)


def dot3(mul, x, high, low):
    x_high, x_low = split(x)
    return mul(x_high, high) + (mul(x_high, low) + mul(x_low, high))


def left3(table, x):
    x_high, x_low = split(x)
    return nn(table, jnp.concatenate([x_high, x_high, x_low], 0))


def rows_forward(v, w):
    low, high = v[:, :256], v[:, 256:]
    return jnp.concatenate([dot3(nn, low + high, w[0], w[1]), dot3(nn, low - high, w[2], w[3])], 1)


def rows_inverse(s, w):
    even, odd = dot3(nt, s[:, :256], w[0], w[1]), dot3(nt, s[:, 256:], w[2], w[3])
    return jnp.concatenate([even + odd, even - odd], 1)


def columns_forward(fields, cs, d8, tw):
    turned = left3(cs, jnp.concatenate(fields, 1))
    tc, ts = tw
    parts = []
    for f in range(len(fields)):
        a, b = turned[:64, 128 * f : 128 * f + 128], turned[64:, 128 * f : 128 * f + 128]
        parts.append(jnp.concatenate([tc * a - ts * b, tc * b + ts * a], 1))
    out = dot3(nn, jnp.concatenate(parts, 0), d8[0], d8[1])
    return [out[64 * f : 64 * f + 64] for f in range(len(fields))]


def columns_inverse(fields, ct, d8, tw):
    out = dot3(nt, jnp.concatenate(fields, 0), d8[0], d8[1])
    tc, ts = tw
    parts = []
    for f in range(len(fields)):
        a, b = out[64 * f : 64 * f + 64, :128], out[64 * f : 64 * f + 64, 128:]
        parts.append(jnp.concatenate([tc * a + ts * b, tc * b - ts * a], 0))
    back = left3(ct, jnp.concatenate(parts, 1))
    return [back[:, 128 * f : 128 * f + 128] for f in range(len(fields))]


def swap_parts(v, roll):
    lane = lax.broadcasted_iota(jnp.int32, v.shape, 1)
    return jnp.where(lane // 8 % 2 == 0, roll(v, v.shape[1] - 8, 1), roll(v, 8, 1))


def part_sign(shape):
    lane = lax.broadcasted_iota(jnp.int32, shape, 1)
    return jnp.where(lane // 8 % 2 == 0, -1.0, 1.0).astype(F32)


def times_ky(v, roll):
    lane = lax.broadcasted_iota(jnp.int32, (1, NG), 1)
    e = lane // 16
    ky = UNIT * (2 * (8 * (e % 16) + lane % 8) + e // 16).astype(F32)
    return part_sign((1, NG)) * ky * swap_parts(v, roll)


def filters(e):
    shape = (64, 128)
    k = lax.broadcasted_iota(jnp.int32, shape, 0)
    lane = lax.broadcasted_iota(jnp.int32, shape, 1)
    mx = k + 64 * (lane // 16)
    my = 2 * (8 * (e % 16) + lane % 8) + e // 16
    kx = UNIT * jnp.where(mx > NG // 2, mx - NG, mx).astype(F32)
    ky = UNIT * my.astype(F32)
    k2 = kx * kx + ky * ky
    safe = jnp.where(k2 > 0, k2, 1.0)
    inverse_sq = jnp.where(k2 > 0, 1.0 / safe, 0.0)
    envelope = jnp.where(mx != NG // 2, AMPLITUDE * jnp.sqrt(k2) / (1.0 + k2), 0.0)
    weight = jnp.where(my == 0, 1.0, 2.0).astype(F32) / (NG * NG)
    base = weight * envelope
    return base, base * kx * inverse_sq, base * kx, base * inverse_sq


def turn_vreg(x, roll):
    row = lax.broadcasted_iota(jnp.int32, (8, 128), 0)
    group = lax.broadcasted_iota(jnp.int32, (8, 128), 1) // 16
    for s in (1, 2, 4):
        row_bit, group_bit = row // s % 2, group // s % 2
        down = roll(roll(x, 8 - s, 0), 16 * s, 1)
        up = down if s == 4 else roll(roll(x, s, 0), 128 - 16 * s, 1)
        x = jnp.where(row_bit == group_bit, x, jnp.where(row_bit == 0, down, up))
    return x


def turn_list(vs, roll):
    group = lax.broadcasted_iota(jnp.int32, vs[0].shape, 1) // 16
    vs = list(vs)
    for s in (1, 2, 4):
        low = group // s % 2 == 0
        for i in range(8):
            if i & s == 0:
                a, b = vs[i], vs[i + s]
                vs[i] = jnp.where(low, a, roll(b, 16 * s, 1))
                vs[i + s] = jnp.where(low, roll(a, 128 - 16 * s, 1), b)
    return vs


def panels(nat, start, stop):
    return jnp.concatenate([nat[72 * eb + start : 72 * eb + stop, :] for eb in range(4)], 1)


def halo_out(backs, roll):
    group = lax.broadcasted_iota(jnp.int32, (32, 128), 1) // 16
    before = after = jnp.zeros((32, 128), F32)
    for f, back in enumerate(backs):
        before = jnp.where(group == 2 * f, roll(back[32:], 16 * ((2 * f - 7) % 8), 1), before)
        shifted = roll(back[:32], 16 * (2 * f + 1), 1)
        after = jnp.where(group == 2 * f + 1, shifted, after)
    return jnp.where(group % 2 == 0, roll(before, 1, 0), roll(after, 31, 0))


def halo_in(mains, halo, roll):
    group = lax.broadcasted_iota(jnp.int32, (32, 128), 1) // 16
    from_next, from_prev = roll(halo, 31, 0), roll(halo, 1, 0)
    out = []
    for f, main in enumerate(mains):
        top = main[:32] + jnp.where(group == 0, roll(from_prev, 16 * ((8 - 2 * f - 1) % 8), 1), 0.0)
        end = main[32:] + jnp.where(group == 7, roll(from_next, 16 * (7 - 2 * f), 1), 0.0)
        out.append(jnp.concatenate([top, end], 0))
    return out


def spread(nat, halo, w, roll):
    rows = [nat[0:48], times_ky(nat[48:64], roll), times_ky(nat[0:16], roll), halo, times_ky(halo, roll)]
    return rows_inverse(jnp.concatenate(rows, 0), w)


def field_rows(out):
    main = (out[0:16], out[16:32], out[32:48], out[48:64], out[64:80])
    edge = (out[80:82], out[82:84], out[84:86], out[94:96], out[88:90])
    return main, edge


def density_of(fields):
    linear, shift_x, slope_x, shift_y, slope_y = fields
    return linear + GROWTH * linear * linear - (shift_x * slope_x + shift_y * slope_y)


def adjoints_of(pulled, fields):
    linear, shift_x, slope_x, shift_y, slope_y = fields
    return (
        pulled * (1.0 + 2.0 * GROWTH * linear),
        -pulled * slope_x,
        -pulled * shift_x,
        -pulled * slope_y,
        -pulled * shift_y,
    )


def adjoint_rows(main, edge, w, roll):
    none = jnp.zeros((2, NG), F32)
    rows = list(main) + [edge[0], edge[1], edge[2], none, edge[4], none, none, edge[3]]
    out = rows_forward(jnp.concatenate(rows, 0), w)
    nat = jnp.concatenate(
        [out[0:16] - times_ky(out[64:80], roll), out[16:48], -times_ky(out[48:64], roll)], 0
    )
    return nat, out[80:88] - times_ky(out[88:96], roll)


def far(i):
    return 8 + jnp.where(i % 2 == 0, i // 2, -(i + 1) // 2)


def plane_peers(gy):
    y, x, core = gy // 8, gy // 2 % 4, gy % 2
    steps = [(dy, dx, dc) for dy in range(4) for dx in range(4) for dc in range(2)][1:]
    steps.sort(key=lambda step: -(min(step[0], 4 - step[0]) + min(step[1], 4 - step[1])))
    return [(y + dy) % 4 * 8 + (x + dx) % 4 * 2 + (core + dc) % 2 for dy, dx, dc in steps]


def kernel(
    n_gx, n_gy, noise_hbm, stencil_hbm, mean_hbm, one_hbm, two_hbm, owner_hbm, depth_hbm, counts_ref,
    w_hbm, cs_hbm, ct_hbm, d8_hbm, tw_hbm, out_ref,
    noise_ref, stencil_ref, mean_ref, one_ref, two_ref, owner_ref, depth_ref,
    w_ref, cs_ref, ct_ref, d8_ref, tw_ref, in_sem,
    s1, r1, s2, r2, s3, r3, s4, r4, nat, field, frame, dsend, dgot, cgot,
    send_sem, recv_sem, zsend_sem, zrecv_sem,
):
    roll = pltpu.roll
    gx, gy = lax.axis_index("gx"), lax.axis_index("gy")

    barrier = pltpu.get_barrier_semaphore()

    @pl.loop(0, n_gx - 1)
    def _(i):
        pl.semaphore_signal(barrier, inc=1, device_id=(lax.rem(gx + far(i), n_gx), gy), device_id_type=MESH)

    for to in plane_peers(gy):
        pl.semaphore_signal(barrier, inc=1, device_id=(gx, to), device_id_type=MESH)

    loads = [
        pltpu.make_async_copy(src, dst, in_sem.at[i])
        for i, (src, dst) in enumerate(
            (
                (noise_hbm, noise_ref), (w_hbm, w_ref), (depth_hbm, depth_ref), (cs_hbm, cs_ref), (ct_hbm, ct_ref),
                (d8_hbm, d8_ref), (tw_hbm, tw_ref), (stencil_hbm, stencil_ref), (mean_hbm, mean_ref),
                (one_hbm, one_ref), (two_hbm, two_ref), (owner_hbm, owner_ref),
            )
        )
    ]
    for load in loads:
        load.start()

    def exchange(phase, src, dst, pitch, count):
        for to in plane_peers(gy):
            pltpu.make_async_remote_copy(
                src_ref=src.at[pl.ds(pl.multiple_of(to * pitch, 8), count)],
                dst_ref=dst.at[pl.ds(pl.multiple_of(gy * pitch, 8), count)],
                send_sem=send_sem.at[phase],
                recv_sem=recv_sem.at[phase],
                device_id=(gx, to),
                device_id_type=MESH,
            ).start()

        mine = pl.ds(pl.multiple_of(gy * pitch, 8), pitch)
        dst[mine, :] = src[mine, :]

    def everything(phase, buf, count):
        rows = pl.ds(0, (n_gy - 1) * count)
        return pltpu.make_async_remote_copy(
            src_ref=buf.at[rows],
            dst_ref=buf.at[rows],
            send_sem=send_sem.at[phase],
            recv_sem=recv_sem.at[phase],
            device_id=(gx, lax.rem(gy + 1, n_gy)),
            device_id_type=MESH,
        )

    loads[0].wait()
    loads[1].wait()
    w = [w_ref[i] for i in range(4)]

    spec = rows_forward(noise_ref[...], w)
    for xh in range(2):
        for eb in range(4):
            block = spec[8 * xh : 8 * xh + 8, 128 * eb : 128 * eb + 128]
            s1[pl.ds(64 * eb + xh, 8, stride=8), :] = turn_vreg(block, roll)
    loads[2].wait()
    left = lax.broadcasted_iota(jnp.int32, (1, 128), 1) < 64
    for other in range(n_gx):
        dsend[other, 0:1, :] = jnp.where(left, depth_ref[2 * other], depth_ref[2 * other + 1])

    pl.semaphore_wait(barrier, n_gy - 1 + n_gx - 1)

    exchange(0, s1, r1, 8, 2)

    def send_counts(start, stop):
        @pl.loop(start, stop)
        def _(i):
            to = lax.rem(gx + far(i), n_gx)
            pltpu.make_async_remote_copy(
                src_ref=counts_ref.at[pl.ds(2 * to, 2)],
                dst_ref=cgot.at[pl.ds(2 * gx, 2)],
                send_sem=zsend_sem.at[0],
                recv_sem=zrecv_sem.at[0],
                device_id=(to, gy),
                device_id_type=MESH,
            ).start()

    send_counts(0, 8)

    @pl.loop(0, n_gx - 1)
    def _(i):
        to = lax.rem(gx + far(i), n_gx)
        pltpu.make_async_remote_copy(
            src_ref=dsend.at[to, pl.ds(0, 1)],
            dst_ref=dgot.at[gx, pl.ds(0, 1)],
            send_sem=zsend_sem.at[1],
            recv_sem=zrecv_sem.at[1],
            device_id=(to, gy),
            device_id_type=MESH,
        ).start()

    own = pltpu.make_async_copy(counts_ref.at[pl.ds(2 * gx, 2)], cgot.at[pl.ds(2 * gx, 2)], zsend_sem.at[2])
    own.start()
    dgot[gx, 0:1, :] = dsend[gx, 0:1, :]

    flt = filters(gy)
    for load in loads[3:]:
        load.wait()
    tw = (tw_ref[0], tw_ref[1])
    d8 = (d8_ref[0], d8_ref[1])
    cs, ct = cs_ref[...], ct_ref[...]
    sign = part_sign((64, 128))

    everything(0, r1, 2).wait_recv()
    packed = jnp.concatenate([r1[pl.ds(xh, 32, stride=8), :] for xh in range(2)], 0)
    modes = columns_forward([packed], cs, d8, tw)[0]
    turned = sign * swap_parts(modes, roll)
    backs = columns_inverse([flt[0] * modes, flt[1] * turned, flt[2] * turned, flt[3] * modes], ct, d8, tw)
    for f in range(4):
        for xh in range(2):
            s2[pl.ds(2 * f + xh, 32, stride=16), :] = backs[f][32 * xh : 32 * xh + 32]
    s2[pl.ds(8, 32, stride=16), :] = halo_out(backs, roll)
    exchange(1, s2, r2, 16, 9)
    send_counts(8, n_gx - 1)

    everything(1, r2, 9).wait_recv()
    for eb in range(4):
        outs = turn_list([r2[128 * eb + 16 * i : 128 * eb + 16 * i + 8, :] for i in range(8)], roll)
        for xl in range(8):
            nat[pl.ds(72 * eb + xl, 8, stride=8), :] = outs[xl]
        nat[72 * eb + 64 : 72 * eb + 72, :] = turn_vreg(r2[pl.ds(128 * eb + 8, 8, stride=16), :], roll)
    field[...] = spread(panels(nat, 0, 64), panels(nat, 64, 72), w, roll)
    main, edge = field_rows(field)
    dens = density_of(main)
    dens_edge = density_of(edge)
    out_ref[1] = dens
    frame[8:24, :] = dens
    frame[7:8, :] = dens_edge[0:1]
    frame[24:25, :] = dens_edge[1:2]
    cols = []
    for b in range(3):
        cols.append(sum(stencil_ref[3 * a + b] * frame[7 + a : 23 + a, :] for a in range(3)))
    smooth = roll(cols[0], 1, 1) + cols[1] + roll(cols[2], NG - 1, 1)

    got = pltpu.make_async_remote_copy(
        src_ref=cgot.at[pl.ds(0, 2 * n_gx - 2)],
        dst_ref=cgot.at[pl.ds(0, 2 * n_gx - 2)],
        send_sem=zsend_sem.at[0],
        recv_sem=zrecv_sem.at[0],
        device_id=(lax.rem(gx + 1, n_gx), gy),
        device_id_type=MESH,
    )
    got_depth = pltpu.make_async_remote_copy(
        src_ref=dgot.at[pl.ds(0, n_gx - 1), pl.ds(0, 1)],
        dst_ref=dgot.at[pl.ds(0, n_gx - 1), pl.ds(0, 1)],
        send_sem=zsend_sem.at[1],
        recv_sem=zrecv_sem.at[1],
        device_id=(lax.rem(gx + 1, n_gx), gy),
        device_id_type=MESH,
    )
    own.wait()
    got.wait_recv()
    got_depth.wait_recv()
    frame[0:8, :] = jnp.zeros((8, NG), F32)
    frame[24:32, :] = jnp.zeros((8, NG), F32)
    for t in range(NT):
        holder = owner_ref[t]
        rank = jnp.int32(0)
        for t2 in range(t):
            rank = rank + jnp.where(owner_ref[t2] == holder, 1, 0)
        seen = cgot[2 * holder + rank].astype(F32)
        classes = dgot[holder]
        row, turned_row = classes[0:1, :], roll(classes, 64, 1)[0:1, :]
        first, second = jnp.where(left, row, turned_row), jnp.where(left, turned_row, row)
        e = jnp.where(rank == 0, first, second)

        def pick(ref):
            out = jnp.full((1, 128), ref[0], F32)
            for value in range(1, 4):
                out = jnp.where(e == value, ref[value], out)
            return out

        level, lin, quad = pick(mean_ref), pick(one_ref), pick(two_ref)
        cell = smooth[:, TC * t : TC * t + TC]
        rate = level * jnp.exp(lin * cell + quad * cell * cell)
        frame[8:24, TC * t : TC * t + TC] = (seen - rate) * (lin + 2.0 * quad * cell)

    cols = []
    for b in range(3):
        inner = sum(stencil_ref[3 * a + b] * frame[9 - a : 25 - a, :] for a in range(3))
        outer = jnp.concatenate([stencil_ref[b] * frame[8:9, :], stencil_ref[6 + b] * frame[23:24, :]], 0)
        cols.append((inner, outer))
    pulled = roll(cols[0][0], NG - 1, 1) + cols[1][0] + roll(cols[2][0], 1, 1)
    pulled_edge = roll(cols[0][1], NG - 1, 1) + cols[1][1] + roll(cols[2][1], 1, 1)
    main, edge = field_rows(field)
    rows, halo = adjoint_rows(adjoints_of(pulled, main), adjoints_of(pulled_edge, edge), w, roll)
    for eb in range(4):
        cols = slice(128 * eb, 128 * eb + 128)
        nat[72 * eb : 72 * eb + 64, :] = rows[:, cols]
        outs = turn_list([nat[pl.ds(72 * eb + xl, 8, stride=8), :] for xl in range(8)], roll)
        for i in range(8):
            s3[128 * eb + 16 * i : 128 * eb + 16 * i + 8, :] = outs[i]
        s3[pl.ds(128 * eb + 8, 8, stride=16), :] = turn_vreg(halo[:, cols], roll)
    exchange(2, s3, r3, 16, 9)

    everything(2, r3, 9).wait_recv()
    mains = [
        jnp.concatenate([r3[pl.ds(2 * f + xh, 32, stride=16), :] for xh in range(2)], 0) for f in range(4)
    ]
    mains = halo_in(mains, r3[pl.ds(8, 32, stride=16), :], roll)
    modes = columns_forward(mains, cs, d8, tw)
    summed = flt[0] * modes[0] + flt[3] * modes[3] - sign * swap_parts(flt[1] * modes[1] + flt[2] * modes[2], roll)
    back = columns_inverse([summed], ct, d8, tw)[0]
    for xh in range(2):
        s4[pl.ds(xh, 32, stride=8), :] = back[32 * xh : 32 * xh + 32]
    exchange(3, s4, r4, 8, 2)

    everything(3, r4, 2).wait_recv()
    for xh in range(2):
        for eb in range(4):
            block = r4[pl.ds(64 * eb + xh, 8, stride=8), :]
            nat[72 * eb + 8 * xh : 72 * eb + 8 * xh + 8, :] = turn_vreg(block, roll)
    out_ref[0] = rows_inverse(panels(nat, 0, 16), w) - noise_ref[...]

    for phase, (buf, count) in enumerate(((s1, 2), (s2, 9), (s3, 9), (s4, 2))):
        everything(phase, buf, count).wait_send()
    got.wait_send()
    got_depth.wait_send()


def local(tables, n_gx, n_gy, noise, stencil, mean_counts, bias_one, bias_two, owner, depth, counts):
    rows = noise.shape[1]
    slots = counts.shape[1]
    vmem = pl.BlockSpec(memory_space=pltpu.VMEM)
    both = pl.pallas_call(
        functools.partial(kernel, n_gx, n_gy),
        out_shape=jax.ShapeDtypeStruct((2, rows, NG), F32),
        in_specs=[pl.BlockSpec(memory_space=pltpu.HBM)] * 13,
        out_specs=pl.BlockSpec(memory_space=pltpu.VMEM),
        scratch_shapes=[
            pltpu.VMEM((rows, NG), F32),
            pltpu.SMEM((9,), F32),
            pltpu.SMEM((4,), F32),
            pltpu.SMEM((4,), F32),
            pltpu.SMEM((4,), F32),
            pltpu.SMEM((NT,), jnp.int32),
            pltpu.SMEM((slots,), jnp.int32),
            *[pltpu.VMEM(table.shape, table.dtype) for table in tables],
            pltpu.SemaphoreType.DMA((12,)),
            pltpu.VMEM((256, 128), F32),
            pltpu.VMEM((256, 128), F32),
            pltpu.VMEM((512, 128), F32),
            pltpu.VMEM((512, 128), F32),
            pltpu.VMEM((512, 128), F32),
            pltpu.VMEM((512, 128), F32),
            pltpu.VMEM((256, 128), F32),
            pltpu.VMEM((256, 128), F32),
            pltpu.VMEM((288, 128), F32),
            pltpu.VMEM((96, NG), F32),
            pltpu.VMEM((32, NG), F32),
            pltpu.VMEM((n_gx, 8, 128), jnp.int32),
            pltpu.VMEM((n_gx, 8, 128), jnp.int32),
            pltpu.VMEM((slots, rows, TC), jnp.int32),
            pltpu.SemaphoreType.DMA((4,)),
            pltpu.SemaphoreType.DMA((4,)),
            pltpu.SemaphoreType.DMA((3,)),
            pltpu.SemaphoreType.DMA((2,)),
        ],
        compiler_params=pltpu.CompilerParams(collective_id=0, has_side_effects=True, vmem_limit_bytes=16 * 1024 * 1024),
        name="posterior",
    )(
        *[
            pltpu.with_memory_space_constraint(x, pltpu.HBM)
            for x in (
                noise.reshape(rows, NG),
                stencil,
                mean_counts,
                bias_one,
                bias_two,
                owner.reshape(-1),
                depth.reshape(slots),
                counts.reshape(slots, rows, TC),
                *[jnp.asarray(table) for table in tables],
            )
        ],
    )
    return both[0:1], both[1:2]


def solution(mesh):
    return jax.shard_map(
        functools.partial(local, make_tables(), mesh.shape["gx"], mesh.shape["gy"]),
        mesh=mesh,
        in_specs=(
            P("gx", "gy", None),
            P(),
            P(),
            P(),
            P(),
            P("gy", "gx", None, None),
            P("gx", None, "gy"),
            P("gx", None, "gy", None, None),
        ),
        out_specs=(P("gx", "gy", None), P("gx", "gy", None)),
        check_vma=False,
    )
```
